256 devices in a mesh: tm: 16 (over x, y_lo, core), batch: 16 (over z, y_hi).
Axes of the slice: x: 4, y: 4 (y_hi: 2, y_lo: 2; y = y_hi * 2 + y_lo), z: 8, core: 2. Of those that a mesh axis runs over, the one named last changes fastest.
Arguments:
- signal: bfloat16 [16, 2048, 4096], P('batch', 'tm'), may hold values from -7.5 to 7.5
- gate_input: bfloat16 [16, 2048, 4096], P('batch', 'tm'), may hold values from -6 to 6
- bc_forward: bfloat16 [16, 2048, 128], P('batch', 'tm'), may hold values from -6 to 6
- bc_backward: bfloat16 [16, 2048, 128], P('batch', 'tm'), may hold values from -6 to 6
- step_raw: bfloat16 [16, 2048, 128], P('batch', 'tm'), may hold values from -12 to 2
- decay_rate: float32 [2, 64], replicated, may hold values from 0.3 to 1
- conv_weight: float32 [2, 4, 4224], replicated, may hold values from -3 to 3
- conv_bias: float32 [2, 4224], replicated, may hold values from -1.5 to 1.5
- skip_gain: float32 [2, 64], replicated, may hold values from 0.5 to 1.5
- norm_gain: float32 [4096], replicated, may hold values from 0.1 to 1.9
Outputs:
- mixed: bfloat16 [16, 2048, 4096], P(None, 'batch', 'tm')
The draws below stay inside these ranges and needn't reach their ends.
All inputs are finite; a program needn't handle non-finite values.
Results may differ from the reference program's by a relative error of at most 0.0075.
Values may be sent and summed in bfloat16 or wider, within the bound.
No kernel may reach another device: no remote copies, remote signals or barrier semaphores. Data moves between devices by JAX's collectives and lax.ppermute only.
A program may use at most 256 MiB of HBM per device.

```python
import math
import jax
import jax.numpy as jnp
from jax import lax

INNER = 4096
HEADDIM = 64
STATE = 64
CONV = 4
GROUP = 128
T_DEV = 128
HEADS = 64
CAPTURE_DURATION = 2048
TRACE_COUNT = 16


def head_classes(key):
    picks = jax.random.uniform(jax.random.fold_in(key, 101), (2, HEADS))
    slow_cut = 0.4
    middle_cut = 0.75
    slow_mask = picks < slow_cut
    middle_mask = (picks >= slow_cut) & (picks < middle_cut)
    return (slow_mask, middle_mask)


def draw_decay_rate(key, part):
    slow_mask, middle_mask = head_classes(key)
    slow_rate = jax.random.uniform(jax.random.fold_in(key, 1), (2, HEADS), jnp.float32, 0.3, 0.6)
    middle_rate = jax.random.uniform(jax.random.fold_in(key, 6), (2, HEADS), jnp.float32, 0.5, 0.7)
    fast_rate = jax.random.uniform(jax.random.fold_in(key, 2), (2, HEADS), jnp.float32, 0.6, 1.0)
    return jnp.where(slow_mask, slow_rate, jnp.where(middle_mask, middle_rate, fast_rate)).astype(jnp.float32)


def draw_step_raw(key, part):
    slow_mask, middle_mask = head_classes(key)
    slow_slots = jnp.concatenate([slow_mask[0], slow_mask[1]])
    middle_slots = jnp.concatenate([middle_mask[0], middle_mask[1]])
    blocks = CAPTURE_DURATION // T_DEV
    noise_jitter = jax.random.uniform(jax.random.fold_in(key, 3), (TRACE_COUNT, CAPTURE_DURATION, 2 * HEADS), jnp.float32, -0.7, 0.7)
    displacement_sizes = jax.random.uniform(jax.random.fold_in(key, 4), (TRACE_COUNT, blocks, 1, 2 * HEADS), jnp.float32, -0.5, 0.5)
    displacement_sizes = jnp.broadcast_to(displacement_sizes, (TRACE_COUNT, blocks, T_DEV, 2 * HEADS)).reshape(TRACE_COUNT, CAPTURE_DURATION, 2 * HEADS)
    resting_floor = jnp.where(slow_slots, math.log(2.0 / CAPTURE_DURATION), jnp.where(middle_slots, math.log(1.1 / T_DEV), math.log(1.6 / T_DEV)))
    spike_moments = jax.random.randint(jax.random.fold_in(key, 5), (TRACE_COUNT, 3), 0, CAPTURE_DURATION)
    spike_trace_picks = jnp.any(jnp.arange(CAPTURE_DURATION)[None, :, None] == spike_moments[:, None, :], axis=-1)
    spike_height = jnp.where(spike_trace_picks[:, :, None] & slow_slots[None, None, :], math.log(0.25 * CAPTURE_DURATION), 0.0)
    combined_waveform = resting_floor[None, None, :] + noise_jitter + displacement_sizes + spike_height
    return combined_waveform.astype(jnp.float32).astype(jnp.bfloat16)


def draw_signal(key, part):
    blocks = CAPTURE_DURATION // T_DEV
    noise_values = jnp.clip(jax.random.normal(jax.random.fold_in(key, 11), (TRACE_COUNT, blocks, T_DEV, INNER), jnp.float32), -6.0, 6.0)
    shard_levels = jnp.exp(jax.random.uniform(jax.random.fold_in(key, 12), (TRACE_COUNT, blocks, 1, 1), jnp.float32, -3.0, 0.2))
    leveled = (noise_values * shard_levels).reshape(TRACE_COUNT, CAPTURE_DURATION, INNER)
    return leveled.astype(jnp.float32).astype(jnp.bfloat16)


def steps_of(key, extent, cuts, smallest, largest):
    gain, own = 1.0, jax.random.fold_in(key, 6)
    for position, blocks in cuts:
        draws = jnp.exp(jax.random.uniform(jax.random.fold_in(own, position), (blocks,), jnp.float32, smallest / len(cuts), largest / len(cuts)))
        gain = gain * jnp.repeat(draws, extent[position] // blocks).reshape([-1 if axis == position else 1 for axis in range(len(extent))])
    return gain


def centred(stream_key, dims, scale, bound, cuts=(), dtype=jnp.bfloat16):
    entries = scale * jax.random.normal(stream_key, dims, jnp.float32)
    if cuts:
        entries = entries * steps_of(stream_key, dims, cuts, -0.22, 0.18)
    return jnp.clip(entries, -bound, bound).astype(dtype)


def setup_inputs(seed: int = 0) -> dict:
    key_list = jax.random.split(jax.random.key(seed), 11)
    return {
        "signal": draw_signal(jax.random.fold_in(key_list[10], 71), 0),
        "gate_input": centred(key_list[1], (TRACE_COUNT, CAPTURE_DURATION, INNER), 1.0, 6.0, ((0, 16), (1, 16))),
        "bc_forward": centred(key_list[2], (TRACE_COUNT, CAPTURE_DURATION, 2 * STATE), 1.0, 6.0, ((0, 16), (1, 16))),
        "bc_backward": centred(key_list[3], (TRACE_COUNT, CAPTURE_DURATION, 2 * STATE), 1.0, 6.0, ((0, 16), (1, 16))),
        "step_raw": draw_step_raw(jax.random.fold_in(key_list[10], 71), 0),
        "decay_rate": draw_decay_rate(jax.random.fold_in(key_list[10], 71), 0),
        "conv_weight": centred(key_list[6], (2, CONV, INNER + 2 * STATE), CONV ** -0.5, 3.0, (), jnp.float32),
        "conv_bias": centred(key_list[7], (2, INNER + 2 * STATE), 0.25, 1.5, (), jnp.float32),
        "skip_gain": jnp.clip(jax.random.uniform(key_list[8], (2, HEADS), jnp.float32, 0.5, 1.5), 0.5, 1.5),
        "norm_gain": jnp.clip(1.0 + 0.18 * jax.random.normal(key_list[9], (INNER,), jnp.float32), 0.1, 1.9),
    }


EPSILON = 1e-05

def conv_silu(sequence, history, weights, offsets):
    length = sequence.shape[0]
    padded = jnp.concatenate([history, sequence], 0).astype(jnp.float32)
    combined_waveform = jnp.broadcast_to(offsets[None, :], (length, sequence.shape[1]))
    for offset in range(weights.shape[0]):
        combined_waveform = combined_waveform + weights[offset][None, :] * padded[offset:offset + length]
    return jax.nn.silu(combined_waveform).astype(jnp.bfloat16)

def block_parts(x_part, b_part, step_size, rate_head):
    log_decay = -step_size * rate_head[None, None, :]
    cum_log = jnp.cumsum(log_decay, axis=1)
    weight_end = jnp.exp(cum_log[:, -1:, :] - cum_log) * step_size
    b_scaled = (b_part.astype(jnp.float32)[:, :, None, :] * weight_end[..., None]).astype(jnp.bfloat16)
    states = jnp.einsum('mqhn,mqhp->mhnp', b_scaled.astype(jnp.float32), x_part.astype(jnp.float32))
    return (cum_log, states, jnp.exp(cum_log[:, -1, :]))

def prepare(x_conv, bc_conv, step_raw, rate_head):
    block_count = x_conv.shape[0] // GROUP
    x_part = x_conv.reshape(block_count, GROUP, -1, HEADDIM)
    b_part = bc_conv[:, :STATE].reshape(block_count, GROUP, STATE)
    c_part = bc_conv[:, STATE:].reshape(block_count, GROUP, STATE)
    step_size = jax.nn.softplus(step_raw.astype(jnp.float32)).reshape(block_count, GROUP, -1)
    cum_log, states, decays = block_parts(x_part, b_part, step_size, rate_head)
    return (x_part, b_part, c_part, step_size, cum_log, states, decays)

def block_outputs(parts, start, skip_head):
    block_len = parts[0].shape[1]
    causal_mask = jnp.arange(block_len)[:, None] >= jnp.arange(block_len)[None, :]

    def advance(state_in, pieces):
        x_block, b_block, c_block, step_block, cum_block, state_block, decay_block = pieces
        scores = jnp.dot(c_block, b_block.T, preferred_element_type=jnp.float32)
        differ = cum_block.T[:, :, None] - cum_block.T[:, None, :]
        masked = jnp.where(causal_mask[None], jnp.exp(jnp.minimum(differ, 0.0)), 0.0)
        mixing = (masked * scores[None] * step_block.T[:, None, :]).astype(jnp.bfloat16)
        local_out = jnp.einsum('hij,jhp->ihp', mixing.astype(jnp.float32), x_block.astype(jnp.float32))
        carried = jnp.einsum('in,hnp->ihp', c_block.astype(jnp.float32), state_in, precision=lax.Precision.HIGHEST)
        result = local_out + jnp.exp(cum_block)[:, :, None] * carried + skip_head[None, :, None] * x_block.astype(jnp.float32)
        new_state = decay_block[:, None, None] * state_in + state_block
        return (new_state, result.astype(jnp.bfloat16))
    _, outputs = lax.scan(advance, start, parts)
    return outputs.reshape(outputs.shape[0] * outputs.shape[1], -1)

def run_direction(signal_seq, bc_seq, step_seq, conv_w, conv_b, rate_head, skip_head):
    rim_rows = conv_w.shape[0] - 1
    x_conv = conv_silu(signal_seq, jnp.zeros((rim_rows, INNER), jnp.bfloat16), conv_w[:, :INNER], conv_b[:INNER])
    bc_conv = conv_silu(bc_seq, jnp.zeros((rim_rows, 2 * STATE), jnp.bfloat16), conv_w[:, INNER:], conv_b[INNER:])
    parts = prepare(x_conv, bc_conv, step_seq, rate_head)
    start = jnp.zeros((HEADS, STATE, HEADDIM), jnp.float32)
    return block_outputs(parts, start, skip_head)

def reference(signal, gate_input, bc_forward, bc_backward, step_raw, decay_rate, conv_weight, conv_bias, skip_gain, norm_gain):

    def one_record(record_args):
        signal_rec, gate_rec, bcf_rec, bcb_rec, step_rec = record_args
        forward_out = run_direction(signal_rec, bcf_rec, step_rec[:, :HEADS], conv_weight[0], conv_bias[0], decay_rate[0], skip_gain[0])
        backward_out = run_direction(signal_rec[::-1], bcb_rec[::-1], step_rec[::-1, HEADS:], conv_weight[1], conv_bias[1], decay_rate[1], skip_gain[1])[::-1]
        gated = (forward_out.astype(jnp.float32) + backward_out.astype(jnp.float32)) * jax.nn.silu(gate_rec.astype(jnp.float32))
        inv_rms = lax.rsqrt(lax.optimization_barrier(jnp.mean(gated * gated, axis=-1, keepdims=True)) + EPSILON)
        return (gated * inv_rms * norm_gain[None, :]).astype(jnp.bfloat16)
    return lax.map(one_record, (signal, gate_input, bc_forward, bc_backward, step_raw))
```

```python
import functools

import jax
import jax.numpy as jnp
from jax import lax
from jax.experimental import pallas as pl
from jax.experimental.pallas import tpu as pltpu
from jax.sharding import PartitionSpec as P

INNER = 4096
HEADDIM = 64
STATE = 64
GROUP = 128
HEADS = 64
BLOCKS = 16
OWN = 4
WIDE = OWN * HEADDIM
ROWS = 2 * GROUP + 8
EPSILON = 1e-05
LOG2E = 1.4426950408889634
VMEM = pl.BlockSpec(memory_space=pltpu.VMEM)
SMEM = pl.BlockSpec(memory_space=pltpu.SMEM)


def pack_kernel(signal, bcf, bcb, step, out):
    both = jnp.concatenate([bcf[0], bcb[0]], axis=1)
    steps = step[0].astype(jnp.float32).T
    for c in range(BLOCKS):
        out[c, :GROUP] = signal[0, :, c * WIDE : (c + 1) * WIDE]
        out[c, GROUP : 2 * GROUP] = both
        mine = jnp.concatenate(
            [steps[c * OWN : (c + 1) * OWN], steps[HEADS + c * OWN : HEADS + (c + 1) * OWN]], axis=0
        )
        out[c, 2 * GROUP :] = jnp.concatenate([mine, jnp.zeros_like(mine)], axis=1).astype(
            jnp.bfloat16
        )


def spread(column, base):
    low = lax.broadcasted_iota(jnp.int32, (GROUP, 128), 1) < HEADDIM
    parts = []
    for p in range(OWN // 2):
        first = column[:, base + 2 * p : base + 2 * p + 1]
        second = column[:, base + 2 * p + 1 : base + 2 * p + 2]
        parts.append(jnp.where(low, first, second))
    return jnp.concatenate(parts, axis=1)


def spread_row(rows, base):
    low = lax.broadcasted_iota(jnp.int32, (1, 128), 1) < HEADDIM
    parts = []
    for p in range(OWN // 2):
        parts.append(
            jnp.where(low, rows[base + 2 * p : base + 2 * p + 1], rows[base + 2 * p + 1 : base + 2 * p + 2])
        )
    return jnp.concatenate(parts, axis=1)


def half_silu(h):
    return h + h * jnp.tanh(h)


def ssm_kernel(
    buf, cw, cb, rate, skip, y, raw, rawbc, cum_s, row_s, end_s, tot_s, x_s, c_s, b_s, carry_s
):
    tm = lax.axis_index("tm")
    col0 = pl.multiple_of(tm * WIDE, WIDE)

    raw_steps = buf[:, 2 * GROUP :, :GROUP].astype(jnp.float32).reshape(BLOCKS * 8, GROUP)
    z = jnp.exp(-jnp.abs(raw_steps))
    u = 1.0 + z
    log1p = jnp.where(u == 1.0, z, jnp.log(u) * (z / jnp.where(u == 1.0, 1.0, u - 1.0)))
    dt = jnp.maximum(raw_steps, 0.0) + log1p
    sub = lax.broadcasted_iota(jnp.int32, (BLOCKS * 8, GROUP), 0) % 8
    rates = jnp.zeros((BLOCKS * 8, GROUP), jnp.float32)
    for k in range(8):
        rates = jnp.where(sub == k, rate[k // OWN, tm * OWN + k % OWN], rates)
    decay = dt * rates * (-LOG2E)
    ri = lax.broadcasted_iota(jnp.int32, (GROUP, GROUP), 0)
    ci = lax.broadcasted_iota(jnp.int32, (GROUP, GROUP), 1)
    prefix = jnp.dot(decay, (ri <= ci).astype(jnp.float32), precision=lax.Precision.HIGHEST)
    suffix = jnp.dot(decay, (ri >= ci).astype(jnp.float32), precision=lax.Precision.HIGHEST)
    is_fwd = sub < OWN
    cum = jnp.where(is_fwd, prefix, suffix)
    total = jnp.where(is_fwd[:, :1], prefix[:, GROUP - 1 :], suffix[:, :1])
    row = cum - jnp.log(dt) * LOG2E
    row_s[...] = row
    tot_s[...] = jnp.broadcast_to(jnp.exp2(total), (BLOCKS * 8, GROUP))
    cum_s[...] = cum.T
    end_s[...] = jnp.exp2(total - row).T

    for ref in (raw, rawbc):
        ref[0:8] = jnp.zeros((8, WIDE), jnp.float32)
        ref[8 + BLOCKS * GROUP :] = jnp.zeros((8, WIDE), jnp.float32)

    def widen(i, _):
        at = pl.ds(pl.multiple_of(8 + i * GROUP, 8), GROUP)
        raw[at] = buf[i, :GROUP].astype(jnp.float32)
        rawbc[at] = buf[i, GROUP : 2 * GROUP].astype(jnp.float32)
        return 0

    lax.fori_loop(0, BLOCKS, widen, 0)

    weights = [[cw[d, pl.ds(k, 1), pl.ds(col0, WIDE)] * 0.5 for k in range(4)] for d in range(2)]
    bias = [cb[pl.ds(d, 1), pl.ds(col0, WIDE)] * 0.5 for d in range(2)]
    weights_bc = [[cw[d, pl.ds(k, 1), INNER:] * 0.5 for k in range(4)] for d in range(2)]
    bias_bc = [cb[pl.ds(d, 1), INNER:] * 0.5 for d in range(2)]
    low = lax.broadcasted_iota(jnp.int32, (GROUP, 128), 1) < STATE

    def shifted(window, s):
        if s == 0:
            return window[8 : 8 + GROUP]
        return pltpu.roll(window, GROUP + 16 - (8 + s), 0)[:GROUP]

    def conv(window, d, taps, offset):
        sign = 1 if d == 0 else -1
        acc = offset + taps[3] * shifted(window, 0)
        for k in range(3):
            acc = acc + taps[k] * shifted(window, sign * (k - 3))
        return half_silu(acc)

    def convolve(i, _):
        at = pl.ds(pl.multiple_of(i * GROUP, GROUP), GROUP + 16)
        window, window_bc = raw[at], rawbc[at]
        for d in range(2):
            x_s[d, i] = conv(window, d, weights[d], bias[d]).astype(jnp.bfloat16)
            bc = conv(window_bc[:, d * 128 : (d + 1) * 128], d, weights_bc[d], bias_bc[d])
            bc = bc.astype(jnp.bfloat16).astype(jnp.float32)
            c_s[d, i] = jnp.where(low, pltpu.roll(bc, STATE, 1), bc).astype(jnp.bfloat16)
            b_s[d, i] = jnp.where(low, bc, 0.0).astype(jnp.bfloat16)
        return 0

    lax.fori_loop(0, BLOCKS, convolve, 0)

    def scan(i, carries):
        new = []
        for d in range(2):
            at = i if d == 0 else BLOCKS - 1 - i
            carry = carries[d]
            high = carry.astype(jnp.bfloat16)
            carry_s[d, at, :STATE] = high
            carry_s[d, at, STATE:] = (carry - high.astype(jnp.float32)).astype(jnp.bfloat16)
            ends = pltpu.roll(end_s[...], (GROUP - 8 * at) % GROUP, 1)
            scaled = (x_s[d, at].astype(jnp.float32) * spread(ends, d * OWN)).astype(jnp.bfloat16)
            state = lax.dot_general(
                b_s[d, at], scaled, (((0,), (0,)), ((), ())), preferred_element_type=jnp.float32
            )[:STATE]
            rows = tot_s[pl.ds(pl.multiple_of(8 * at, 8), 8)]
            new.append(spread_row(rows, d * OWN) * carry + state)
        return tuple(new)

    zero = jnp.zeros((STATE, WIDE), jnp.float32)
    lax.fori_loop(0, BLOCKS, scan, (zero, zero))

    lane = lax.broadcasted_iota(jnp.int32, (1, WIDE), 1) // HEADDIM
    skips = []
    for d in range(2):
        value = jnp.zeros((1, WIDE), jnp.float32)
        for h in range(OWN):
            value = jnp.where(lane == h, skip[d, tm * OWN + h], value)
        skips.append(value)

    def outputs(i, _):
        cums = pltpu.roll(cum_s[...], (GROUP - 8 * i) % GROUP, 1)
        rows = row_s[pl.ds(pl.multiple_of(8 * i, 8), 8)]
        decays = jnp.exp2(cums)
        x = [x_s[d, i] for d in range(2)]
        wide = jnp.zeros((GROUP, WIDE), jnp.float32)
        scores = []
        for d in range(2):
            score = lax.dot_general(
                c_s[d, i], b_s[d, i], (((1,), (1,)), ((), ())), preferred_element_type=jnp.float32
            )
            scores.append(jnp.where((ri >= ci) if d == 0 else (ri <= ci), score, 0.0))
            carried = jnp.dot(c_s[d, i], carry_s[d, i], preferred_element_type=jnp.float32)
            wide = wide + carried * spread(decays, d * OWN) + skips[d] * x[d].astype(jnp.float32)
        for p in range(OWN // 2):
            left, right = [], []
            for q in range(2):
                for d in range(2):
                    k = d * OWN + 2 * p + q
                    grow = jnp.exp2(jnp.minimum(cums[:, k : k + 1] - rows[k : k + 1], 64.0))
                    left.append((grow * scores[d]).astype(jnp.bfloat16))
                    pair = x[d][:, p * 128 : (p + 1) * 128]
                    keep = low if q == 0 else jnp.logical_not(low)
                    right.append(jnp.where(keep, pair, jnp.zeros_like(pair)))
            local = jnp.dot(
                jnp.concatenate(left, axis=1),
                jnp.concatenate(right, axis=0),
                preferred_element_type=jnp.float32,
            )
            y[i, :, p * 128 : (p + 1) * 128] = local + wide[:, p * 128 : (p + 1) * 128]
        return 0

    lax.fori_loop(0, BLOCKS, outputs, 0)


def gate_kernel(y, gate, gated, sums):
    def one(i, _):
        g = y[i] * half_silu(gate[i].astype(jnp.float32) * 0.5)
        gated[i] = g
        total = lax.dot_general(
            jnp.ones((8, WIDE), jnp.float32),
            g * g,
            (((1,), (1,)), ((), ())),
            precision=lax.Precision.HIGHEST,
            preferred_element_type=jnp.float32,
        )
        sums[:, pl.ds(i, 1), :] = jnp.broadcast_to(total[:1][None], (BLOCKS, 1, GROUP))
        return 0

    lax.fori_loop(0, BLOCKS, one, 0)


def norm_kernel(gated, sums, gain, out, inv_s):
    gains = gain[0:1, pl.ds(pl.multiple_of(lax.axis_index("tm") * WIDE, WIDE), WIDE)]
    total = sums[0]
    for k in range(1, BLOCKS):
        total = total + sums[k]
    inv = lax.rsqrt(total * (1.0 / INNER) + EPSILON)
    inv_s[...] = jnp.concatenate(
        [inv, jnp.zeros((GROUP - BLOCKS, GROUP), jnp.float32)], axis=0
    ).T

    def one(i, _):
        scale = pltpu.roll(inv_s[...], (GROUP - i) % GROUP, 1)[:, :1]
        out[i] = (gated[i] * scale * gains).astype(jnp.bfloat16)
        return 0

    lax.fori_loop(0, BLOCKS, one, 0)


def swap(array, axis):
    return lax.all_to_all(array, axis, split_axis=0, concat_axis=0, tiled=True)


def shards(
    signal,
    gate_input,
    bc_forward,
    bc_backward,
    step_raw,
    decay_rate,
    conv_weight,
    conv_bias,
    skip_gain,
    norm_gain,
):
    f32, bf16 = jnp.float32, jnp.bfloat16
    packed = pl.pallas_call(
        pack_kernel,
        out_shape=jax.ShapeDtypeStruct((BLOCKS, ROWS, WIDE), bf16),
        in_specs=[VMEM] * 4,
        out_specs=VMEM,
        name="pack",
        cost_estimate=pl.CostEstimate(flops=0, bytes_accessed=4 << 20, transcendentals=0),
    )(signal, bc_forward, bc_backward, step_raw)
    got = swap(packed, "tm")
    gates = gate_input[0].reshape(GROUP, BLOCKS, WIDE).transpose(1, 0, 2)
    gates = swap(gates, "tm")
    y = pl.pallas_call(
        ssm_kernel,
        out_shape=jax.ShapeDtypeStruct((BLOCKS, GROUP, WIDE), f32),
        in_specs=[VMEM, VMEM, VMEM, SMEM, SMEM],
        out_specs=VMEM,
        scratch_shapes=[
            pltpu.VMEM((BLOCKS * GROUP + 16, WIDE), f32),
            pltpu.VMEM((BLOCKS * GROUP + 16, WIDE), f32),
            pltpu.VMEM((GROUP, BLOCKS * 8), f32),
            pltpu.VMEM((BLOCKS * 8, GROUP), f32),
            pltpu.VMEM((GROUP, BLOCKS * 8), f32),
            pltpu.VMEM((BLOCKS * 8, GROUP), f32),
            pltpu.VMEM((2, BLOCKS, GROUP, WIDE), bf16),
            pltpu.VMEM((2, BLOCKS, GROUP, 128), bf16),
            pltpu.VMEM((2, BLOCKS, GROUP, 128), bf16),
            pltpu.VMEM((2, BLOCKS, 2 * STATE, WIDE), bf16),
        ],
        name="ssm",
        cost_estimate=pl.CostEstimate(
            flops=20_000_000_000, bytes_accessed=8 << 20, transcendentals=4_000_000
        ),
    )(got, conv_weight, conv_bias, decay_rate, skip_gain)
    gated, sums = pl.pallas_call(
        gate_kernel,
        out_shape=(
            jax.ShapeDtypeStruct((BLOCKS, GROUP, WIDE), f32),
            jax.ShapeDtypeStruct((BLOCKS, BLOCKS, GROUP), f32),
        ),
        in_specs=[VMEM] * 2,
        out_specs=(VMEM, VMEM),
        name="gate",
    )(y, gates)
    sums = swap(sums, "tm")
    normed = pl.pallas_call(
        norm_kernel,
        out_shape=jax.ShapeDtypeStruct((BLOCKS, GROUP, WIDE), bf16),
        in_specs=[VMEM] * 3,
        out_specs=VMEM,
        scratch_shapes=[pltpu.VMEM((GROUP, GROUP), f32)],
        name="norm",
    )(gated, sums, norm_gain[None])
    return swap(normed, "batch")


def solution(mesh):
    in_specs = (
        P("batch", "tm", None),
        P("batch", "tm", None),
        P("batch", "tm", None),
        P("batch", "tm", None),
        P("batch", "tm", None),
        P(),
        P(),
        P(),
        P(),
        P(),
    )
    out_specs = P(None, "batch", "tm")
    return jax.shard_map(shards, mesh=mesh, in_specs=in_specs, out_specs=out_specs, check_vma=False)
```

```python
import functools

import jax
import jax.numpy as jnp
from jax import lax
from jax.experimental import pallas as pl
from jax.experimental.pallas import tpu as pltpu
from jax.sharding import PartitionSpec as P

INNER = 4096
HEADDIM = 64
STATE = 64
GROUP = 128
HEADS = 64
BLOCKS = 16
OWN = 4
WIDE = OWN * HEADDIM
ROWS = 2 * GROUP + 8
EPSILON = 1e-05
UNROLL_BC, UNROLL_X, UNROLL_Y = 2, 2, 2
LOG2E = 1.4426950408889634
VMEM = pl.BlockSpec(memory_space=pltpu.VMEM)
SMEM = pl.BlockSpec(memory_space=pltpu.SMEM)


def pack_kernel(signal, bcf, bcb, step, out):
    both = jnp.concatenate([bcf[0], bcb[0]], axis=1)
    steps = step[0].astype(jnp.float32).T
    for c in range(BLOCKS):
        out[c, :GROUP] = signal[0, :, c * WIDE : (c + 1) * WIDE]
        out[c, GROUP : 2 * GROUP] = both
        mine = jnp.concatenate(
            [steps[c * OWN : (c + 1) * OWN], steps[HEADS + c * OWN : HEADS + (c + 1) * OWN]], axis=0
        )
        out[c, 2 * GROUP :] = jnp.concatenate([mine, jnp.zeros_like(mine)], axis=1).astype(
            jnp.bfloat16
        )


def half_silu(h):
    return h + h * jnp.tanh(h)


def pieces(value):
    parts = []
    for _ in range(3):
        part = value.astype(jnp.bfloat16).astype(jnp.float32)
        parts.append(part)
        value = value - part
    return parts


def ssm_kernel(
    buf, cw, cb, rate, skip, y, raw, row_s, cum_s, dec_s, end_s, tot_s, fixed_s, x_s, c_s, bt_s, btb_s, st_s, carry_s
):
    f32, bf16 = jnp.float32, jnp.bfloat16
    tm = lax.axis_index("tm")
    n8 = BLOCKS * 8

    raw_steps = buf[:, 2 * GROUP :, :GROUP].astype(f32).reshape(n8, GROUP)
    z = jnp.exp(-jnp.abs(raw_steps))
    u = 1.0 + z
    log1p = jnp.where(u == 1.0, z, jnp.log(u) * (z / jnp.where(u == 1.0, 1.0, u - 1.0)))
    dt = jnp.maximum(raw_steps, 0.0) + log1p
    sub = lax.broadcasted_iota(jnp.int32, (8, GROUP), 0)
    rates = jnp.zeros((8, GROUP), f32)
    for k in range(8):
        rates = jnp.where(sub == k, rate[k // OWN, tm * OWN + k % OWN], rates)
    decay = (dt.reshape(BLOCKS, 8, GROUP) * (rates * (-LOG2E))[None]).reshape(n8, GROUP)
    ri = lax.broadcasted_iota(jnp.int32, (GROUP, GROUP), 0)
    ci = lax.broadcasted_iota(jnp.int32, (GROUP, GROUP), 1)
    sums = jnp.concatenate([(ri <= ci).astype(f32), (ri >= ci).astype(f32)], axis=1).astype(bf16)
    both = jnp.dot(
        jnp.concatenate(pieces(decay), axis=1).astype(bf16),
        jnp.concatenate([sums] * 3, axis=0),
        preferred_element_type=f32,
    )
    prefix, suffix = both[:, :GROUP], both[:, GROUP:]
    is_fwd = lax.broadcasted_iota(jnp.int32, (n8, GROUP), 0) % 8 < OWN
    cum = jnp.where(is_fwd, prefix, suffix)
    total = jnp.where(is_fwd[:, :1], prefix[:, GROUP - 1 :], suffix[:, :1])
    row = cum - jnp.log(dt) * LOG2E
    row_s[...] = -row
    cum_s[...] = cum
    dec_s[...] = jnp.exp2(cum)
    end_s[...] = jnp.exp2(total - row)
    tot_s[...] = jnp.broadcast_to(jnp.exp2(total), (n8, GROUP))

    low = lax.broadcasted_iota(jnp.int32, (GROUP, 128), 1) < HEADDIM
    sub128 = lax.broadcasted_iota(jnp.int32, (96, 128), 0)
    for k in range(12):
        if k < 8:
            chosen = (sub128 < 24) & (sub128 % 8 == k)
        else:
            d, p = divmod(k - 8, 2)
            head = d * OWN + 2 * p + jnp.where(low[:96], 0, 1)
            chosen = (sub128 >= 32) & (sub128 < 56) & (sub128 % 8 == head)
        fixed_s[k] = jnp.where(chosen, 1.0, 0.0).astype(bf16)

    for t in range(4):
        raw[t, 0:8] = jnp.zeros((8, 128), f32)
        raw[t, 8 + BLOCKS * GROUP :] = jnp.zeros((8, 128), f32)

    def widen(i, _):
        at = pl.ds(pl.multiple_of(8 + i * GROUP, 8), GROUP)
        for t in range(4):
            top = (t // 2) * GROUP
            raw[t, at] = buf[i, top : top + GROUP, (t % 2) * 128 : (t % 2 + 1) * 128].astype(f32)
        return 0

    lax.fori_loop(0, BLOCKS, widen, 0)

    def conv(t, i, d, taps, offset):
        sign = 1 if d == 0 else -1
        acc = offset
        for k in range(4):
            acc = acc + taps[k] * raw[t, pl.ds(i * GROUP + (8 + sign * (k - 3)), GROUP)]
        return half_silu(acc)

    def taps_of(d, lanes):
        return [cw[d, pl.ds(k, 1), lanes] * 0.5 for k in range(4)], cb[pl.ds(d, 1), lanes] * 0.5

    for d in range(2):
        taps, offset = taps_of(d, slice(INNER, INNER + 128))

        def convolve_bc(j, _):
            for e in range(UNROLL_BC):
                i = j * UNROLL_BC + e
                bc = conv(2 + d, i, d, taps, offset).astype(bf16).astype(f32)
                c_s[d, i] = jnp.where(low, pltpu.roll(bc, STATE, 1), bc).astype(bf16)
                turned = bc.T[:STATE]
                bt_s[d, i] = turned
                btb_s[d, i] = turned.astype(bf16)
            return 0

        lax.fori_loop(0, BLOCKS // UNROLL_BC, convolve_bc, 0)

    for p in range(OWN // 2):
        lanes = pl.ds(pl.multiple_of(tm * WIDE + p * 128, 128), 128)
        filters = [taps_of(d, lanes) for d in range(2)]

        def convolve(j, _):
            for e in range(UNROLL_X):
                i = j * UNROLL_X + e
                ends = end_s[pl.ds(pl.multiple_of(8 * i, 8), 8)]
                for d in range(2):
                    x = conv(p, i, d, *filters[d]).astype(bf16)
                    x_s[d, p, i] = x
                    k = d * OWN + 2 * p
                    turned = bt_s[d, i]
                    scaled = jnp.concatenate(
                        [turned * ends[k : k + 1], turned * ends[k + 1 : k + 2]], axis=0
                    ).astype(bf16)
                    state = jnp.dot(scaled, x, preferred_element_type=f32)
                    st_s[d, p, i] = jnp.where(low[:STATE], state[:STATE], state[STATE:])
            return 0

        lax.fori_loop(0, BLOCKS // UNROLL_X, convolve, 0)

    def scan(i, carries):
        new = []
        for d in range(2):
            at = i if d == 0 else BLOCKS - 1 - i
            rows = tot_s[pl.ds(pl.multiple_of(8 * at, 8), 8)]
            for p in range(OWN // 2):
                carry = carries[2 * d + p]
                high = carry.astype(bf16)
                lanes = slice(p * 128, (p + 1) * 128)
                carry_s[d, at, :STATE, lanes] = high
                carry_s[d, at, STATE:, lanes] = (carry - high.astype(f32)).astype(bf16)
                k = d * OWN + 2 * p
                keep = jnp.where(low[:1], rows[k : k + 1], rows[k + 1 : k + 2])
                new.append(keep * carry + st_s[d, p, at])
        return tuple(new)

    lax.fori_loop(0, BLOCKS, scan, tuple(jnp.zeros((STATE, 128), f32) for _ in range(4)))

    skips = []
    for d in range(2):
        for p in range(OWN // 2):
            at = tm * OWN + 2 * p
            skips.append(jnp.where(low[:1], skip[d, at], skip[d, at + 1]))
    sub32 = lax.broadcasted_iota(jnp.int32, (32, GROUP), 0)
    ones = jnp.where(sub32 < 24, 1.0, 0.0)
    blank = jnp.zeros((8, GROUP), f32)

    def one_block(i):
        at = pl.ds(pl.multiple_of(8 * i, 8), 8)
        left = jnp.concatenate(
            [ones, *pieces(cum_s[at]), blank, *pieces(dec_s[at]), blank, jnp.zeros((32, GROUP), f32)],
            axis=0,
        ).T.astype(bf16)
        rows = jnp.concatenate([*pieces(row_s[at]), blank], axis=0)
        right = []
        for k in range(12):
            part = jnp.where(sub32 % 8 == k, rows, 0.0) if k < 8 else jnp.zeros((32, GROUP), f32)
            right.append(jnp.concatenate([part.astype(bf16), fixed_s[k]], axis=0))
        grid = jnp.dot(left, jnp.concatenate(right, axis=1), preferred_element_type=f32)
        scores, wide = [], [0.0, 0.0]
        for d in range(2):
            c = c_s[d, i]
            score = jnp.dot(c[:, :STATE], btb_s[d, i], preferred_element_type=f32)
            scores.append(jnp.where((ri >= ci) if d == 0 else (ri <= ci), score, 0.0))
            carried = jnp.dot(c, carry_s[d, i], preferred_element_type=f32)
            for p in range(OWN // 2):
                lanes = slice(p * 128, (p + 1) * 128)
                decays = grid[:, (8 + 2 * d + p) * 128 : (9 + 2 * d + p) * 128]
                wide[p] = (
                    wide[p] + carried[:, lanes] * decays + skips[2 * d + p] * x_s[d, p, i].astype(f32)
                )
        for p in range(OWN // 2):
            heads = []
            for q in range(2):
                parts = []
                for d in range(2):
                    k = d * OWN + 2 * p + q
                    grow = jnp.exp2(jnp.minimum(grid[:, k * 128 : (k + 1) * 128], 64.0))
                    parts.append((grow * scores[d]).astype(bf16))
                heads.append(jnp.concatenate(parts, axis=1))
            local = jnp.dot(
                jnp.concatenate(heads, axis=0),
                jnp.concatenate([x_s[0, p, i], x_s[1, p, i]], axis=0),
                preferred_element_type=f32,
            )
            local = jnp.where(low, local[:GROUP], local[GROUP:])
            y[i, :, p * 128 : (p + 1) * 128] = local + wide[p]

    def outputs(j, _):
        for e in range(UNROLL_Y):
            one_block(j * UNROLL_Y + e)
        return 0

    lax.fori_loop(0, BLOCKS // UNROLL_Y, outputs, 0)


def gate_kernel(y, gate, gated, sums):
    def one(i, _):
        g = y[i] * half_silu(gate[i].astype(jnp.float32) * 0.5)
        gated[i] = g
        total = lax.dot_general(
            jnp.ones((8, WIDE), jnp.float32),
            g * g,
            (((1,), (1,)), ((), ())),
            precision=lax.Precision.HIGHEST,
            preferred_element_type=jnp.float32,
        )
        sums[:, pl.ds(i, 1), :] = jnp.broadcast_to(total[:1][None], (BLOCKS, 1, GROUP))
        return 0

    lax.fori_loop(0, BLOCKS, one, 0)


def norm_kernel(gated, sums, gain, out, inv_s):
    gains = gain[0:1, pl.ds(pl.multiple_of(lax.axis_index("tm") * WIDE, WIDE), WIDE)]
    total = sums[0]
    for k in range(1, BLOCKS):
        total = total + sums[k]
    inv = lax.rsqrt(total * (1.0 / INNER) + EPSILON)
    inv_s[...] = jnp.concatenate(
        [inv, jnp.zeros((GROUP - BLOCKS, GROUP), jnp.float32)], axis=0
    ).T

    def one(i, _):
        scale = pltpu.roll(inv_s[...], (GROUP - i) % GROUP, 1)[:, :1]
        out[i] = (gated[i] * scale * gains).astype(jnp.bfloat16)
        return 0

    lax.fori_loop(0, BLOCKS, one, 0)


def swap(array, axis):
    return lax.all_to_all(array, axis, split_axis=0, concat_axis=0, tiled=True)


def shards(
    signal,
    gate_input,
    bc_forward,
    bc_backward,
    step_raw,
    decay_rate,
    conv_weight,
    conv_bias,
    skip_gain,
    norm_gain,
):
    f32, bf16 = jnp.float32, jnp.bfloat16
    packed = pl.pallas_call(
        pack_kernel,
        out_shape=jax.ShapeDtypeStruct((BLOCKS, ROWS, WIDE), bf16),
        in_specs=[VMEM] * 4,
        out_specs=VMEM,
        name="pack",
        cost_estimate=pl.CostEstimate(flops=0, bytes_accessed=4 << 20, transcendentals=0),
    )(signal, bc_forward, bc_backward, step_raw)
    got = swap(packed, "tm")
    gates = gate_input[0].reshape(GROUP, BLOCKS, WIDE).transpose(1, 0, 2)
    gates = swap(gates, "tm")
    y = pl.pallas_call(
        ssm_kernel,
        out_shape=jax.ShapeDtypeStruct((BLOCKS, GROUP, WIDE), f32),
        in_specs=[VMEM, VMEM, VMEM, SMEM, SMEM],
        out_specs=VMEM,
        scratch_shapes=[
            pltpu.VMEM((4, BLOCKS * GROUP + 16, 128), f32),
            *[pltpu.VMEM((BLOCKS * 8, GROUP), f32)] * 5,
            pltpu.VMEM((12, 96, 128), bf16),
            pltpu.VMEM((2, 2, BLOCKS, GROUP, 128), bf16),
            pltpu.VMEM((2, BLOCKS, GROUP, 128), bf16),
            pltpu.VMEM((2, BLOCKS, STATE, 128), f32),
            pltpu.VMEM((2, BLOCKS, STATE, 128), bf16),
            pltpu.VMEM((2, 2, BLOCKS, STATE, 128), f32),
            pltpu.VMEM((2, BLOCKS, 2 * STATE, WIDE), bf16),
        ],
        name="ssm",
        cost_estimate=pl.CostEstimate(
            flops=20_000_000_000, bytes_accessed=8 << 20, transcendentals=4_000_000
        ),
    )(got, conv_weight, conv_bias, decay_rate, skip_gain)
    gated, sums = pl.pallas_call(
        gate_kernel,
        out_shape=(
            jax.ShapeDtypeStruct((BLOCKS, GROUP, WIDE), f32),
            jax.ShapeDtypeStruct((BLOCKS, BLOCKS, GROUP), f32),
        ),
        in_specs=[VMEM] * 2,
        out_specs=(VMEM, VMEM),
        name="gate",
    )(y, gates)
    sums = swap(sums, "tm")
    normed = pl.pallas_call(
        norm_kernel,
        out_shape=jax.ShapeDtypeStruct((BLOCKS, GROUP, WIDE), bf16),
        in_specs=[VMEM] * 3,
        out_specs=VMEM,
        scratch_shapes=[pltpu.VMEM((GROUP, GROUP), f32)],
        name="norm",
    )(gated, sums, norm_gain[None])
    return swap(normed, "batch")


def solution(mesh):
    in_specs = (
        P("batch", "tm", None),
        P("batch", "tm", None),
        P("batch", "tm", None),
        P("batch", "tm", None),
        P("batch", "tm", None),
        P(),
        P(),
        P(),
        P(),
        P(),
    )
    out_specs = P(None, "batch", "tm")
    return jax.shard_map(shards, mesh=mesh, in_specs=in_specs, out_specs=out_specs, check_vma=False)
```

```python
import functools

import jax
import jax.numpy as jnp
from jax import lax
from jax.experimental import pallas as pl
from jax.experimental.pallas import tpu as pltpu
from jax.sharding import PartitionSpec as P

INNER = 4096
HEADDIM = 64
STATE = 64
GROUP = 128
HEADS = 64
BLOCKS = 16
OWN = 4
WIDE = OWN * HEADDIM
HALF = GROUP // 2
ROWS = GROUP + HALF + 8
EPSILON = 1e-05
UNROLL_BC, UNROLL_X, UNROLL_Y = 8, 8, 4
LOG2E = 1.4426950408889634
VMEM = pl.BlockSpec(memory_space=pltpu.VMEM)
LIMIT = pltpu.CompilerParams(vmem_limit_bytes=32 << 20)
SMEM = pl.BlockSpec(memory_space=pltpu.SMEM)


def pack_kernel(signal, bcf, bcb, step, out, turned):
    turned[...] = step[0].astype(jnp.float32).T
    at = pl.multiple_of(pl.program_id(0) * 4 * OWN, 4 * OWN)
    forward, backward = turned[pl.ds(at, 4 * OWN)], turned[pl.ds(HEADS + at, 4 * OWN)]
    for e in range(4):
        out[e, :GROUP] = signal[0, :, e * WIDE : (e + 1) * WIDE]
        bc = (bcf if e % 2 == 0 else bcb)[0]
        out[e, GROUP : GROUP + HALF] = jnp.concatenate([bc[:HALF], bc[HALF:]], axis=1)
        mine = jnp.concatenate(
            [forward[e * OWN : (e + 1) * OWN], backward[e * OWN : (e + 1) * OWN]], axis=0
        )
        out[e, GROUP + HALF :] = jnp.concatenate([mine, jnp.zeros_like(mine)], axis=1).astype(
            jnp.bfloat16
        )


def half_silu(h):
    return h + h * jnp.tanh(h)


def pieces(value):
    parts = []
    for _ in range(3):
        part = value.astype(jnp.bfloat16).astype(jnp.float32)
        parts.append(part)
        value = value - part
    return parts


def ssm_kernel(
    buf, other, cw, cb, rate, skip, y, ybuf, sent, raw, row_s, cum_s, dec_s, end_s, tot_s, fixed_s, x_s, c_s, bt_s, btb_s, st_s, carry_s
):
    f32, bf16 = jnp.float32, jnp.bfloat16
    tm = lax.axis_index("tm")
    n8 = BLOCKS * 8

    raw_steps = buf[:, GROUP + HALF :, :GROUP].astype(f32).reshape(n8, GROUP)
    z = jnp.exp(-jnp.abs(raw_steps))
    u = 1.0 + z
    log1p = jnp.where(u == 1.0, z, jnp.log(u) * (z / jnp.where(u == 1.0, 1.0, u - 1.0)))
    dt = jnp.maximum(raw_steps, 0.0) + log1p
    sub = lax.broadcasted_iota(jnp.int32, (8, GROUP), 0)
    rates = jnp.zeros((8, GROUP), f32)
    for k in range(8):
        rates = jnp.where(sub == k, rate[k // OWN, tm * OWN + k % OWN], rates)
    decay = (dt.reshape(BLOCKS, 8, GROUP) * (rates * (-LOG2E))[None]).reshape(n8, GROUP)
    ri = lax.broadcasted_iota(jnp.int32, (GROUP, GROUP), 0)
    ci = lax.broadcasted_iota(jnp.int32, (GROUP, GROUP), 1)
    sums = jnp.concatenate([(ri <= ci).astype(f32), (ri >= ci).astype(f32)], axis=1).astype(bf16)
    both = jnp.dot(
        jnp.concatenate(pieces(decay), axis=1).astype(bf16),
        jnp.concatenate([sums] * 3, axis=0),
        preferred_element_type=f32,
    )
    prefix, suffix = both[:, :GROUP], both[:, GROUP:]
    is_fwd = lax.broadcasted_iota(jnp.int32, (n8, GROUP), 0) % 8 < OWN
    cum = jnp.where(is_fwd, prefix, suffix)
    total = jnp.where(is_fwd[:, :1], prefix[:, GROUP - 1 :], suffix[:, :1])
    row = cum - jnp.log(dt) * LOG2E
    row_s[...] = -row
    cum_s[...] = cum
    dec_s[...] = jnp.exp2(cum)
    end_s[...] = jnp.exp2(total - row)
    tot_s[...] = jnp.broadcast_to(jnp.exp2(total), (n8, GROUP))

    low = lax.broadcasted_iota(jnp.int32, (GROUP, 128), 1) < HEADDIM
    sub128 = lax.broadcasted_iota(jnp.int32, (96, 128), 0)
    for k in range(12):
        if k < 8:
            chosen = (sub128 < 24) & (sub128 % 8 == k)
        else:
            d, p = divmod(k - 8, 2)
            head = d * OWN + 2 * p + jnp.where(low[:96], 0, 1)
            chosen = (sub128 >= 32) & (sub128 < 56) & (sub128 % 8 == head)
        fixed_s[k] = jnp.where(chosen, 1.0, 0.0).astype(bf16)

    for t in range(4):
        raw[t, 0:8] = jnp.zeros((8, 128), f32)
        raw[t, 8 + BLOCKS * GROUP :] = jnp.zeros((8, 128), f32)

    even = lax.rem(tm, 2) == 0

    def widen(i, _):
        at = pl.multiple_of(8 + i * GROUP, 8)
        for t in range(2):
            raw[t, pl.ds(at, GROUP)] = buf[i, :GROUP, t * 128 : (t + 1) * 128].astype(f32)
            near = buf[i, GROUP : GROUP + HALF, t * 128 : (t + 1) * 128].astype(f32)
            far = other[i, :, t * 128 : (t + 1) * 128].astype(f32)
            raw[2, pl.ds(at + t * HALF, HALF)] = jnp.where(even, near, far)
            raw[3, pl.ds(at + t * HALF, HALF)] = jnp.where(even, far, near)
        return 0

    lax.fori_loop(0, BLOCKS, widen, 0)

    def conv(t, i, d, taps, offset):
        sign = 1 if d == 0 else -1
        acc = offset
        for k in range(4):
            acc = acc + taps[k] * raw[t, pl.ds(i * GROUP + (8 + sign * (k - 3)), GROUP)]
        return half_silu(acc)

    def taps_of(d, lanes):
        return [cw[d, pl.ds(k, 1), lanes] * 0.5 for k in range(4)], cb[pl.ds(d, 1), lanes] * 0.5

    for d in range(2):
        taps, offset = taps_of(d, slice(INNER, INNER + 128))

        def convolve_bc(j, _):
            for e in range(UNROLL_BC):
                i = j * UNROLL_BC + e
                bc = conv(2 + d, i, d, taps, offset).astype(bf16).astype(f32)
                c_s[d, i] = jnp.where(low, pltpu.roll(bc, STATE, 1), bc).astype(bf16)
                turned = bc.T[:STATE]
                bt_s[d, i] = turned
                btb_s[d, i] = turned.astype(bf16)
            return 0

        lax.fori_loop(0, BLOCKS // UNROLL_BC, convolve_bc, 0)

    for p in range(OWN // 2):
        lanes = pl.ds(pl.multiple_of(tm * WIDE + p * 128, 128), 128)
        filters = [taps_of(d, lanes) for d in range(2)]

        def convolve(j, _):
            for e in range(UNROLL_X):
                i = j * UNROLL_X + e
                ends = end_s[pl.ds(pl.multiple_of(8 * i, 8), 8)]
                for d in range(2):
                    x = conv(p, i, d, *filters[d]).astype(bf16)
                    x_s[d, p, i] = x
                    k = d * OWN + 2 * p
                    turned = bt_s[d, i]
                    scaled = jnp.concatenate(
                        [turned * ends[k : k + 1], turned * ends[k + 1 : k + 2]], axis=0
                    ).astype(bf16)
                    state = jnp.dot(scaled, x, preferred_element_type=f32)
                    st_s[d, p, i] = jnp.where(low[:STATE], state[:STATE], state[STATE:])
            return 0

        lax.fori_loop(0, BLOCKS // UNROLL_X, convolve, 0)

    def scan(i, carries):
        new = []
        for d in range(2):
            at = i if d == 0 else BLOCKS - 1 - i
            rows = tot_s[pl.ds(pl.multiple_of(8 * at, 8), 8)]
            for p in range(OWN // 2):
                carry = carries[2 * d + p]
                high = carry.astype(bf16)
                lanes = slice(p * 128, (p + 1) * 128)
                carry_s[d, at, :STATE, lanes] = high
                carry_s[d, at, STATE:, lanes] = (carry - high.astype(f32)).astype(bf16)
                k = d * OWN + 2 * p
                keep = jnp.where(low[:1], rows[k : k + 1], rows[k + 1 : k + 2])
                new.append(keep * carry + st_s[d, p, at])
        return tuple(new)

    lax.fori_loop(0, BLOCKS, scan, tuple(jnp.zeros((STATE, 128), f32) for _ in range(4)))

    skips = []
    for d in range(2):
        for p in range(OWN // 2):
            at = tm * OWN + 2 * p
            skips.append(jnp.where(low[:1], skip[d, at], skip[d, at + 1]))
    sub32 = lax.broadcasted_iota(jnp.int32, (32, GROUP), 0)
    ones = jnp.where(sub32 < 24, 1.0, 0.0)
    blank = jnp.zeros((8, GROUP), f32)

    def one_block(i):
        at = pl.ds(pl.multiple_of(8 * i, 8), 8)
        left = jnp.concatenate(
            [ones, *pieces(cum_s[at]), blank, *pieces(dec_s[at]), blank, jnp.zeros((32, GROUP), f32)],
            axis=0,
        ).T.astype(bf16)
        rows = jnp.concatenate([*pieces(row_s[at]), blank], axis=0)
        right = []
        for k in range(12):
            part = jnp.where(sub32 % 8 == k, rows, 0.0) if k < 8 else jnp.zeros((32, GROUP), f32)
            right.append(jnp.concatenate([part.astype(bf16), fixed_s[k]], axis=0))
        grid = jnp.dot(left, jnp.concatenate(right, axis=1), preferred_element_type=f32)
        scores, wide = [], [0.0, 0.0]
        for d in range(2):
            c = c_s[d, i]
            score = jnp.dot(c[:, :STATE], btb_s[d, i], preferred_element_type=f32)
            scores.append(jnp.where((ri >= ci) if d == 0 else (ri <= ci), score, 0.0))
            carried = jnp.dot(c, carry_s[d, i], preferred_element_type=f32)
            for p in range(OWN // 2):
                lanes = slice(p * 128, (p + 1) * 128)
                decays = grid[:, (8 + 2 * d + p) * 128 : (9 + 2 * d + p) * 128]
                wide[p] = (
                    wide[p] + carried[:, lanes] * decays + skips[2 * d + p] * x_s[d, p, i].astype(f32)
                )
        for p in range(OWN // 2):
            heads = []
            for q in range(2):
                parts = []
                for d in range(2):
                    k = d * OWN + 2 * p + q
                    grow = jnp.exp2(jnp.minimum(grid[:, k * 128 : (k + 1) * 128], 64.0))
                    parts.append((grow * scores[d]).astype(bf16))
                heads.append(jnp.concatenate(parts, axis=1))
            local = jnp.dot(
                jnp.concatenate(heads, axis=0),
                jnp.concatenate([x_s[0, p, i], x_s[1, p, i]], axis=0),
                preferred_element_type=f32,
            )
            local = jnp.where(low, local[:GROUP], local[GROUP:])
            ybuf[i, :, p * 128 : (p + 1) * 128] = local + wide[p]

    def send(j):
        at = pl.ds(j * UNROLL_Y, UNROLL_Y)
        return pltpu.make_async_copy(ybuf.at[at], y.at[at], sent.at[j])

    def outputs(j, _):
        @pl.when(j > 0)
        def _():
            send(j - 1).start()

        for e in range(UNROLL_Y):
            one_block(j * UNROLL_Y + e)
        return 0

    count = BLOCKS // UNROLL_Y
    lax.fori_loop(0, count, outputs, 0)
    send(count - 1).start()
    for j in range(count):
        send(j).wait()


def gate_kernel(y, gate, gated, sums, ybuf, came):
    f32, bf16 = jnp.float32, jnp.bfloat16

    def fetch(j):
        at = pl.ds(j * 4, 4)
        return pltpu.make_async_copy(y.at[at], ybuf.at[at], came.at[j])

    for j in range(BLOCKS // 4):
        fetch(j).start()

    def four(j, _):
        fetch(j).wait()
        for e in range(4):
            i = j * 4 + e
            g = ybuf[i] * half_silu(gate[i].astype(f32) * 0.5)
            gated[i] = g
            square = g * g
            square = square[:, :128] + square[:, 128:]
            high = square.astype(bf16)
            parts = jnp.concatenate([high, (square - high.astype(f32)).astype(bf16)], axis=1)
            total = lax.dot_general(
                jnp.ones((8, WIDE), bf16), parts, (((1,), (1,)), ((), ())), preferred_element_type=f32
            )
            sums[:, pl.ds(i, 1), :] = jnp.broadcast_to(total[:1][None], (BLOCKS, 1, GROUP))
        return 0

    lax.fori_loop(0, BLOCKS // 4, four, 0)


def norm_kernel(gated, sums, gain, out):
    gains = gain[0:1, pl.ds(pl.multiple_of(lax.axis_index("tm") * WIDE, WIDE), WIDE)]
    total = sums[0]
    for k in range(1, BLOCKS):
        total = total + sums[k]
    inv = lax.rsqrt(total * (1.0 / INNER) + EPSILON)
    columns = jnp.concatenate([inv, jnp.zeros((GROUP - BLOCKS, GROUP), jnp.float32)], axis=0).T
    for i in range(BLOCKS):
        out[i] = (gated[i] * columns[:, i : i + 1] * gains).astype(jnp.bfloat16)


def local(array):
    return pltpu.with_memory_space_constraint(array, pltpu.VMEM)


def swap(array, axis):
    return lax.all_to_all(array, axis, split_axis=0, concat_axis=0, tiled=True)


def shards(
    signal,
    gate_input,
    bc_forward,
    bc_backward,
    step_raw,
    decay_rate,
    conv_weight,
    conv_bias,
    skip_gain,
    norm_gain,
):
    f32, bf16 = jnp.float32, jnp.bfloat16
    packed = pl.pallas_call(
        pack_kernel,
        grid=(4,),
        out_shape=jax.ShapeDtypeStruct((BLOCKS, ROWS, WIDE), bf16),
        in_specs=[
            pl.BlockSpec((1, GROUP, 4 * WIDE), lambda i: (0, 0, i)),
            *[pl.BlockSpec((1, GROUP, 128), lambda i: (0, 0, 0))] * 3,
        ],
        out_specs=pl.BlockSpec((4, ROWS, WIDE), lambda i: (i, 0, 0)),
        scratch_shapes=[pltpu.VMEM((GROUP, 128), f32)],
        name="pack",
        cost_estimate=pl.CostEstimate(flops=0, bytes_accessed=3 << 20, transcendentals=0),
    )(signal, bc_forward, bc_backward, step_raw)
    gates = gate_input[0].reshape(GROUP, BLOCKS, WIDE).transpose(1, 0, 2)
    got, gates = lax.optimization_barrier((swap(packed, "tm"), gates))
    other = lax.ppermute(
        got[:, GROUP : GROUP + HALF], "tm", [(i, i ^ 1) for i in range(BLOCKS)]
    )
    gates = swap(gates, "tm")
    y = pl.pallas_call(
        ssm_kernel,
        out_shape=pltpu.HBM((BLOCKS, GROUP, WIDE), f32),
        compiler_params=LIMIT,
        in_specs=[VMEM, VMEM, VMEM, VMEM, SMEM, SMEM],
        out_specs=pl.BlockSpec(memory_space=pl.ANY),
        scratch_shapes=[
            pltpu.VMEM((BLOCKS, GROUP, WIDE), f32),
            pltpu.SemaphoreType.DMA((BLOCKS // UNROLL_Y,)),
            pltpu.VMEM((4, BLOCKS * GROUP + 16, 128), f32),
            *[pltpu.VMEM((BLOCKS * 8, GROUP), f32)] * 5,
            pltpu.VMEM((12, 96, 128), bf16),
            pltpu.VMEM((2, 2, BLOCKS, GROUP, 128), bf16),
            pltpu.VMEM((2, BLOCKS, GROUP, 128), bf16),
            pltpu.VMEM((2, BLOCKS, STATE, 128), f32),
            pltpu.VMEM((2, BLOCKS, STATE, 128), bf16),
            pltpu.VMEM((2, 2, BLOCKS, STATE, 128), f32),
            pltpu.VMEM((2, BLOCKS, 2 * STATE, WIDE), bf16),
        ],
        name="ssm",
        cost_estimate=pl.CostEstimate(
            flops=20_000_000_000, bytes_accessed=8 << 20, transcendentals=4_000_000
        ),
    )(local(got), local(other), conv_weight, conv_bias, decay_rate, skip_gain)
    gated, sums = pl.pallas_call(
        gate_kernel,
        out_shape=(
            pltpu.VMEM((BLOCKS, GROUP, WIDE), f32),
            pltpu.VMEM((BLOCKS, BLOCKS, GROUP), f32),
        ),
        compiler_params=LIMIT,
        in_specs=[pl.BlockSpec(memory_space=pl.ANY), VMEM],
        out_specs=(VMEM, VMEM),
        scratch_shapes=[
            pltpu.VMEM((BLOCKS, GROUP, WIDE), f32),
            pltpu.SemaphoreType.DMA((BLOCKS // 4,)),
        ],
        name="gate",
    )(pltpu.with_memory_space_constraint(y, pltpu.HBM), local(gates))
    sums = swap(sums, "tm")
    normed = pl.pallas_call(
        norm_kernel,
        out_shape=pltpu.VMEM((BLOCKS, GROUP, WIDE), bf16),
        compiler_params=LIMIT,
        in_specs=[VMEM] * 3,
        out_specs=VMEM,
        name="norm",
    )(local(gated), local(sums), norm_gain[None])
    return swap(normed, "batch")


def solution(mesh):
    in_specs = (
        P("batch", "tm", None),
        P("batch", "tm", None),
        P("batch", "tm", None),
        P("batch", "tm", None),
        P("batch", "tm", None),
        P(),
        P(),
        P(),
        P(),
        P(),
    )
    out_specs = P(None, "batch", "tm")
    return jax.shard_map(shards, mesh=mesh, in_specs=in_specs, out_specs=out_specs, check_vma=False)
```

```python
import jax
import jax.numpy as jnp
from jax import lax
from jax.experimental import pallas as pl
from jax.experimental.pallas import tpu as pltpu
from jax.sharding import PartitionSpec as P


INNER = 4096
HEADDIM = 64
STATE = 64
GROUP = 128
HEADS = 64
BLOCKS = 16
OWN = 4
WIDE = OWN * HEADDIM
HALF = GROUP // 2
ROWS = GROUP + HALF + 8
EARLY, LATE = (2,), (0, 1, 3)
EPSILON = 1e-05
UNROLL_BC, UNROLL_X, UNROLL_Y = 8, 8, 4
LOG2E = 1.4426950408889634
VMEM = pl.BlockSpec(memory_space=pltpu.VMEM)
LIMIT = pltpu.CompilerParams(vmem_limit_bytes=32 << 20)
ANY = pl.BlockSpec(memory_space=pl.ANY)
SMEM = pl.BlockSpec(memory_space=pltpu.SMEM)


def pack_kernel(signal, bcf, bcb, step, out, buf, bc, steps, came, small, sent):
    def fetch(c):
        source = signal.at[0, :, pl.ds(c * WIDE, WIDE)]
        return pltpu.make_async_copy(source, buf.at[c, pl.ds(0, GROUP)], came.at[c])

    def send(c):
        return pltpu.make_async_copy(buf.at[c], out.at[c], sent.at[c])

    sides = [
        pltpu.make_async_copy(step.at[0], steps, small.at[0]),
        pltpu.make_async_copy(bcf.at[0], bc.at[0], small.at[1]),
        pltpu.make_async_copy(bcb.at[0], bc.at[1], small.at[2]),
    ]
    for side in sides:
        side.start()
    for c in range(BLOCKS):
        fetch(c).start()
    for side in sides:
        side.wait()
    folded = [jnp.concatenate([bc[d, :HALF], bc[d, HALF:]], axis=1) for d in range(2)]
    turned = steps[...].astype(jnp.float32).T
    for c in range(BLOCKS):
        buf[c, GROUP : GROUP + HALF] = folded[c % 2]
        mine = jnp.concatenate(
            [turned[c * OWN : (c + 1) * OWN], turned[HEADS + c * OWN : HEADS + (c + 1) * OWN]], axis=0
        )
        buf[c, GROUP + HALF :] = jnp.concatenate([mine, jnp.zeros_like(mine)], axis=1).astype(
            jnp.bfloat16
        )
    for c in range(BLOCKS):
        fetch(c).wait()
        send(c).start()
    for c in range(BLOCKS):
        send(c).wait()


def half_silu(h):
    return h + h * jnp.tanh(h)


def pieces(value):
    parts = []
    for _ in range(3):
        part = value.astype(jnp.bfloat16).astype(jnp.float32)
        parts.append(part)
        value = value - part
    return parts


def ssm_kernel(
    buf, other, cw, cb, rate, skip, y, ybuf, sent, raw, row_s, cum_s, dec_s, end_s, tot_s, fixed_s, x_s, c_s, bt_s, btb_s, st_s, carry_s
):
    f32, bf16 = jnp.float32, jnp.bfloat16
    tm = lax.axis_index("tm")
    n8 = BLOCKS * 8

    raw_steps = buf[:, GROUP + HALF :, :GROUP].astype(f32).reshape(n8, GROUP)
    z = jnp.exp(-jnp.abs(raw_steps))
    u = 1.0 + z
    log1p = jnp.where(u == 1.0, z, jnp.log(u) * (z / jnp.where(u == 1.0, 1.0, u - 1.0)))
    dt = jnp.maximum(raw_steps, 0.0) + log1p
    sub = lax.broadcasted_iota(jnp.int32, (8, GROUP), 0)
    rates = jnp.zeros((8, GROUP), f32)
    for k in range(8):
        rates = jnp.where(sub == k, rate[k // OWN, tm * OWN + k % OWN], rates)
    decay = (dt.reshape(BLOCKS, 8, GROUP) * (rates * (-LOG2E))[None]).reshape(n8, GROUP)
    ri = lax.broadcasted_iota(jnp.int32, (GROUP, GROUP), 0)
    ci = lax.broadcasted_iota(jnp.int32, (GROUP, GROUP), 1)
    sums = jnp.concatenate([(ri <= ci).astype(f32), (ri >= ci).astype(f32)], axis=1).astype(bf16)
    both = jnp.dot(
        jnp.concatenate(pieces(decay), axis=1).astype(bf16),
        jnp.concatenate([sums] * 3, axis=0),
        preferred_element_type=f32,
    )
    prefix, suffix = both[:, :GROUP], both[:, GROUP:]
    is_fwd = lax.broadcasted_iota(jnp.int32, (n8, GROUP), 0) % 8 < OWN
    cum = jnp.where(is_fwd, prefix, suffix)
    total = jnp.where(is_fwd[:, :1], prefix[:, GROUP - 1 :], suffix[:, :1])
    row = cum - jnp.log(dt) * LOG2E
    row_s[...] = -row
    cum_s[...] = cum
    dec_s[...] = jnp.exp2(cum)
    end_s[...] = jnp.exp2(total - row)
    tot_s[...] = jnp.broadcast_to(jnp.exp2(total), (n8, GROUP))

    low = lax.broadcasted_iota(jnp.int32, (GROUP, 128), 1) < HEADDIM
    sub128 = lax.broadcasted_iota(jnp.int32, (96, 128), 0)
    for k in range(12):
        if k < 8:
            chosen = (sub128 < 24) & (sub128 % 8 == k)
        else:
            d, p = divmod(k - 8, 2)
            head = d * OWN + 2 * p + jnp.where(low[:96], 0, 1)
            chosen = (sub128 >= 32) & (sub128 < 56) & (sub128 % 8 == head)
        fixed_s[k] = jnp.where(chosen, 1.0, 0.0).astype(bf16)

    for t in range(4):
        raw[t, 0:8] = jnp.zeros((8, 128), f32)
        raw[t, 8 + BLOCKS * GROUP :] = jnp.zeros((8, 128), f32)

    even = lax.rem(tm, 2) == 0

    def widen(i, _):
        at = pl.multiple_of(8 + i * GROUP, 8)
        for t in range(2):
            raw[t, pl.ds(at, GROUP)] = buf[i, :GROUP, t * 128 : (t + 1) * 128].astype(f32)
            near = buf[i, GROUP : GROUP + HALF, t * 128 : (t + 1) * 128].astype(f32)
            far = other[i, :, t * 128 : (t + 1) * 128].astype(f32)
            raw[2, pl.ds(at + t * HALF, HALF)] = jnp.where(even, near, far)
            raw[3, pl.ds(at + t * HALF, HALF)] = jnp.where(even, far, near)
        return 0

    lax.fori_loop(0, BLOCKS, widen, 0)

    def conv(t, i, d, taps, offset):
        sign = 1 if d == 0 else -1
        acc = offset
        for k in range(4):
            acc = acc + taps[k] * raw[t, pl.ds(i * GROUP + (8 + sign * (k - 3)), GROUP)]
        return half_silu(acc)

    def taps_of(d, lanes):
        return [cw[d, pl.ds(k, 1), lanes] * 0.5 for k in range(4)], cb[pl.ds(d, 1), lanes] * 0.5

    for d in range(2):
        taps, offset = taps_of(d, slice(INNER, INNER + 128))

        def convolve_bc(j, _):
            for e in range(UNROLL_BC):
                i = j * UNROLL_BC + e
                bc = conv(2 + d, i, d, taps, offset).astype(bf16).astype(f32)
                c_s[d, i] = jnp.where(low, pltpu.roll(bc, STATE, 1), bc).astype(bf16)
                turned = bc.T[:STATE]
                bt_s[d, i] = turned
                btb_s[d, i] = turned.astype(bf16)
            return 0

        lax.fori_loop(0, BLOCKS // UNROLL_BC, convolve_bc, 0)

    for p in range(OWN // 2):
        lanes = pl.ds(pl.multiple_of(tm * WIDE + p * 128, 128), 128)
        filters = [taps_of(d, lanes) for d in range(2)]

        def convolve(j, _):
            for e in range(UNROLL_X):
                i = j * UNROLL_X + e
                ends = end_s[pl.ds(pl.multiple_of(8 * i, 8), 8)]
                for d in range(2):
                    x = conv(p, i, d, *filters[d]).astype(bf16)
                    x_s[d, p, i] = x
                    k = d * OWN + 2 * p
                    turned = bt_s[d, i]
                    scaled = jnp.concatenate(
                        [turned * ends[k : k + 1], turned * ends[k + 1 : k + 2]], axis=0
                    ).astype(bf16)
                    state = jnp.dot(scaled, x, preferred_element_type=f32)
                    st_s[d, p, i] = jnp.where(low[:STATE], state[:STATE], state[STATE:])
            return 0

        lax.fori_loop(0, BLOCKS // UNROLL_X, convolve, 0)

    def scan(i, carries):
        new = []
        for d in range(2):
            at = i if d == 0 else BLOCKS - 1 - i
            rows = tot_s[pl.ds(pl.multiple_of(8 * at, 8), 8)]
            for p in range(OWN // 2):
                carry = carries[2 * d + p]
                high = carry.astype(bf16)
                lanes = slice(p * 128, (p + 1) * 128)
                carry_s[d, at, :STATE, lanes] = high
                carry_s[d, at, STATE:, lanes] = (carry - high.astype(f32)).astype(bf16)
                k = d * OWN + 2 * p
                keep = jnp.where(low[:1], rows[k : k + 1], rows[k + 1 : k + 2])
                new.append(keep * carry + st_s[d, p, at])
        return tuple(new)

    lax.fori_loop(0, BLOCKS, scan, tuple(jnp.zeros((STATE, 128), f32) for _ in range(4)))

    skips = []
    for d in range(2):
        for p in range(OWN // 2):
            at = tm * OWN + 2 * p
            skips.append(jnp.where(low[:1], skip[d, at], skip[d, at + 1]))
    sub32 = lax.broadcasted_iota(jnp.int32, (32, GROUP), 0)
    ones = jnp.where(sub32 < 24, 1.0, 0.0)
    blank = jnp.zeros((8, GROUP), f32)

    def one_block(i):
        at = pl.ds(pl.multiple_of(8 * i, 8), 8)
        left = jnp.concatenate(
            [ones, *pieces(cum_s[at]), blank, *pieces(dec_s[at]), blank, jnp.zeros((32, GROUP), f32)],
            axis=0,
        ).T.astype(bf16)
        rows = jnp.concatenate([*pieces(row_s[at]), blank], axis=0)
        right = []
        for k in range(12):
            part = jnp.where(sub32 % 8 == k, rows, 0.0) if k < 8 else jnp.zeros((32, GROUP), f32)
            right.append(jnp.concatenate([part.astype(bf16), fixed_s[k]], axis=0))
        grid = jnp.dot(left, jnp.concatenate(right, axis=1), preferred_element_type=f32)
        scores, wide = [], [0.0, 0.0]
        for d in range(2):
            c = c_s[d, i]
            score = jnp.dot(c[:, :STATE], btb_s[d, i], preferred_element_type=f32)
            scores.append(jnp.where((ri >= ci) if d == 0 else (ri <= ci), score, 0.0))
            carried = jnp.dot(c, carry_s[d, i], preferred_element_type=f32)
            for p in range(OWN // 2):
                lanes = slice(p * 128, (p + 1) * 128)
                decays = grid[:, (8 + 2 * d + p) * 128 : (9 + 2 * d + p) * 128]
                wide[p] = (
                    wide[p] + carried[:, lanes] * decays + skips[2 * d + p] * x_s[d, p, i].astype(f32)
                )
        for p in range(OWN // 2):
            heads = []
            for q in range(2):
                parts = []
                for d in range(2):
                    k = d * OWN + 2 * p + q
                    grow = jnp.exp2(jnp.minimum(grid[:, k * 128 : (k + 1) * 128], 64.0))
                    parts.append((grow * scores[d]).astype(bf16))
                heads.append(jnp.concatenate(parts, axis=1))
            local = jnp.dot(
                jnp.concatenate(heads, axis=0),
                jnp.concatenate([x_s[0, p, i], x_s[1, p, i]], axis=0),
                preferred_element_type=f32,
            )
            local = jnp.where(low, local[:GROUP], local[GROUP:])
            ybuf[i, :, p * 128 : (p + 1) * 128] = local + wide[p]

    def send(j):
        at = pl.ds(j * UNROLL_Y, UNROLL_Y)
        return pltpu.make_async_copy(ybuf.at[at], y.at[at], sent.at[j])

    def outputs(j, _):
        @pl.when(j > 0)
        def _():
            send(j - 1).start()

        for e in range(UNROLL_Y):
            one_block(j * UNROLL_Y + e)
        return 0

    count = BLOCKS // UNROLL_Y
    lax.fori_loop(0, count, outputs, 0)
    send(count - 1).start()
    for j in range(count):
        send(j).wait()


def gate_kernel(y, gate, gated, sums, out, wide, ybuf, came, sent):
    f32, bf16 = jnp.float32, jnp.bfloat16

    def fetch(j):
        at = pl.ds(j * 4, 4)
        return pltpu.make_async_copy(y.at[at], ybuf.at[at], came.at[j])

    def send(j):
        at = pl.ds(j * 4, 4)
        return pltpu.make_async_copy(out.at[at], gated.at[at], sent.at[j])

    for j in range(BLOCKS // 4):
        fetch(j).start()

    def four(j, _):
        @pl.when(j > 0)
        def _():
            send(j - 1).start()

        for e in range(4):
            i = j * 4 + e
            wide[i] = half_silu(gate[i].astype(f32) * 0.5)
        fetch(j).wait()
        for e in range(4):
            i = j * 4 + e
            g = ybuf[i] * wide[i]
            out[i] = g.astype(bf16)
            square = g * g
            square = square[:, :128] + square[:, 128:]
            high = square.astype(bf16)
            parts = jnp.concatenate([high, (square - high.astype(f32)).astype(bf16)], axis=1)
            total = lax.dot_general(
                jnp.ones((8, WIDE), bf16), parts, (((1,), (1,)), ((), ())), preferred_element_type=f32
            )
            sums[pl.ds(i, 1)] = total[:1]
        return 0

    lax.fori_loop(0, BLOCKS // 4, four, 0)
    send(BLOCKS // 4 - 1).start()
    for j in range(BLOCKS // 4):
        send(j).wait()


def norm_kernel(gated, total, gain, target, out, sent):
    gains = gain[0:1, pl.ds(pl.multiple_of(lax.axis_index("tm") * WIDE, WIDE), WIDE)]
    inv = lax.rsqrt(total[...] * (1.0 / INNER) + EPSILON)
    columns = jnp.concatenate([inv, jnp.zeros((GROUP - BLOCKS, GROUP), jnp.float32)], axis=0).T

    def send(j):
        at = pl.ds(j * 4, 4)
        return pltpu.make_async_copy(out.at[at], target.at[at], sent.at[j])

    for j in range(BLOCKS // 4):
        if j > 0:
            send(j - 1).start()
        for i in range(4 * j, 4 * j + 4):
            wide = gated[i].astype(jnp.float32) * columns[:, i : i + 1] * gains
            out[i] = wide.astype(jnp.bfloat16)
    send(BLOCKS // 4 - 1).start()
    for j in range(BLOCKS // 4):
        send(j).wait()


def total_of(sums):
    for moves in (
        [[i ^ b for i in range(BLOCKS)] for b in (1, 2, 3)],
        [[(i + b) % BLOCKS for i in range(BLOCKS)] for b in (4, 8, 12)],
    ):
        came = [lax.ppermute(sums, "tm", list(enumerate(move))) for move in moves]
        sums = sums + came[0] + came[1] + came[2]
    return sums


def turned_over(rows, bits):
    mine = lax.axis_index("batch")
    for b in bits:
        pairs = rows.reshape(BLOCKS >> (b + 1), 2, 1 << b, GROUP)
        upper = (mine >> b) & 1 == 1
        give = jnp.where(upper, pairs[:, 0], pairs[:, 1])
        got = lax.ppermute(give, "batch", [(i, i ^ (1 << b)) for i in range(BLOCKS)])
        pairs = [jnp.where(upper, got, pairs[:, 0]), jnp.where(upper, pairs[:, 1], got)]
        rows = jnp.stack(pairs, axis=1).reshape(BLOCKS, GROUP)
    return rows


def far(array):
    return pltpu.with_memory_space_constraint(array, pltpu.HBM)


def local(array):
    return pltpu.with_memory_space_constraint(array, pltpu.VMEM)


def swap(array, axis):
    return lax.all_to_all(array, axis, split_axis=0, concat_axis=0, tiled=True)


def shards(
    signal,
    gate_input,
    bc_forward,
    bc_backward,
    step_raw,
    decay_rate,
    conv_weight,
    conv_bias,
    skip_gain,
    norm_gain,
):
    f32, bf16 = jnp.float32, jnp.bfloat16
    packed = pl.pallas_call(
        pack_kernel,
        out_shape=pltpu.HBM((BLOCKS, ROWS, WIDE), bf16),
        in_specs=[ANY] * 4,
        out_specs=ANY,
        scratch_shapes=[
            pltpu.VMEM((BLOCKS, ROWS, WIDE), bf16),
            pltpu.VMEM((2, GROUP, 128), bf16),
            pltpu.VMEM((GROUP, 128), bf16),
            pltpu.SemaphoreType.DMA((BLOCKS,)),
            pltpu.SemaphoreType.DMA((3,)),
            pltpu.SemaphoreType.DMA((BLOCKS,)),
        ],
        name="pack",
        cost_estimate=pl.CostEstimate(flops=0, bytes_accessed=3 << 20, transcendentals=0),
    )(*[far(a) for a in (signal, bc_forward, bc_backward, step_raw)])
    gates = gate_input[0].reshape(GROUP, BLOCKS, WIDE).transpose(1, 0, 2)
    got, gates = lax.optimization_barrier((swap(packed, "tm"), gates))
    other = lax.ppermute(
        got[:, GROUP : GROUP + HALF], "tm", [(i, i ^ 1) for i in range(BLOCKS)]
    )
    gates = swap(gates, "tm")
    y = pl.pallas_call(
        ssm_kernel,
        out_shape=pltpu.HBM((BLOCKS, GROUP, WIDE), f32),
        compiler_params=LIMIT,
        in_specs=[VMEM, VMEM, VMEM, VMEM, SMEM, SMEM],
        out_specs=ANY,
        scratch_shapes=[
            pltpu.VMEM((BLOCKS, GROUP, WIDE), f32),
            pltpu.SemaphoreType.DMA((BLOCKS // UNROLL_Y,)),
            pltpu.VMEM((4, BLOCKS * GROUP + 16, 128), f32),
            *[pltpu.VMEM((BLOCKS * 8, GROUP), f32)] * 5,
            pltpu.VMEM((12, 96, 128), bf16),
            pltpu.VMEM((2, 2, BLOCKS, GROUP, 128), bf16),
            pltpu.VMEM((2, BLOCKS, GROUP, 128), bf16),
            pltpu.VMEM((2, BLOCKS, STATE, 128), f32),
            pltpu.VMEM((2, BLOCKS, STATE, 128), bf16),
            pltpu.VMEM((2, 2, BLOCKS, STATE, 128), f32),
            pltpu.VMEM((2, BLOCKS, 2 * STATE, WIDE), bf16),
        ],
        name="ssm",
        cost_estimate=pl.CostEstimate(
            flops=20_000_000_000, bytes_accessed=8 << 20, transcendentals=4_000_000
        ),
    )(local(got), local(other), conv_weight, conv_bias, decay_rate, skip_gain)
    gated, sums = pl.pallas_call(
        gate_kernel,
        out_shape=(
            pltpu.HBM((BLOCKS, GROUP, WIDE), bf16),
            pltpu.VMEM((BLOCKS, GROUP), f32),
        ),
        compiler_params=LIMIT,
        in_specs=[ANY, VMEM],
        out_specs=(ANY, VMEM),
        scratch_shapes=[
            pltpu.VMEM((BLOCKS, GROUP, WIDE), bf16),
            pltpu.VMEM((BLOCKS, GROUP, WIDE), f32),
            pltpu.VMEM((BLOCKS, GROUP, WIDE), f32),
            pltpu.SemaphoreType.DMA((BLOCKS // 4,)),
            pltpu.SemaphoreType.DMA((BLOCKS // 4,)),
        ],
        name="gate",
    )(far(y), local(gates))
    sums = turned_over(sums, EARLY)
    gated = swap(gated, "batch")
    sums = total_of(sums)
    sums = turned_over(sums, LATE)
    return pl.pallas_call(
        norm_kernel,
        out_shape=pltpu.HBM((BLOCKS, GROUP, WIDE), bf16),
        in_specs=[VMEM] * 3,
        out_specs=ANY,
        scratch_shapes=[
            pltpu.VMEM((BLOCKS, GROUP, WIDE), bf16),
            pltpu.SemaphoreType.DMA((BLOCKS // 4,)),
        ],
        compiler_params=LIMIT,
        name="norm",
    )(local(gated), sums, norm_gain[None])


def solution(mesh):
    in_specs = (
        P("batch", "tm", None),
        P("batch", "tm", None),
        P("batch", "tm", None),
        P("batch", "tm", None),
        P("batch", "tm", None),
        P(),
        P(),
        P(),
        P(),
        P(),
    )
    out_specs = P(None, "batch", "tm")
    return jax.shard_map(shards, mesh=mesh, in_specs=in_specs, out_specs=out_specs, check_vma=False)
```

```python
import jax
import jax.numpy as jnp
from jax import lax
from jax.experimental import pallas as pl
from jax.experimental.pallas import tpu as pltpu
from jax.sharding import PartitionSpec as P


INNER = 4096
HEADDIM = 64
STATE = 64
GROUP = 128
HEADS = 64
BLOCKS = 16
OWN = 4
WIDE = OWN * HEADDIM
HALF = GROUP // 2
ROWS = GROUP + HALF + 8
EARLY, LATE = (2,), (0, 1, 3)
EPSILON = 1e-05
UNROLL_BC, UNROLL_X, UNROLL_Y = 8, 8, 4
LOG2E = 1.4426950408889634
VMEM = pl.BlockSpec(memory_space=pltpu.VMEM)
LIMIT = pltpu.CompilerParams(vmem_limit_bytes=32 << 20)
ANY = pl.BlockSpec(memory_space=pl.ANY)
SMEM = pl.BlockSpec(memory_space=pltpu.SMEM)


def pack_kernel(signal, bcf, bcb, step, out, buf, bc, steps, came, small, sent):
    def fetch(c):
        source = signal.at[0, :, pl.ds(c * WIDE, WIDE)]
        return pltpu.make_async_copy(source, buf.at[c, pl.ds(0, GROUP)], came.at[c])

    def send(c):
        return pltpu.make_async_copy(buf.at[c], out.at[c], sent.at[c])

    sides = [
        pltpu.make_async_copy(step.at[0], steps, small.at[0]),
        pltpu.make_async_copy(bcf.at[0], bc.at[0], small.at[1]),
        pltpu.make_async_copy(bcb.at[0], bc.at[1], small.at[2]),
    ]
    for side in sides:
        side.start()
    for c in range(BLOCKS):
        fetch(c).start()
    for side in sides:
        side.wait()
    folded = [jnp.concatenate([bc[d, :HALF], bc[d, HALF:]], axis=1) for d in range(2)]
    turned = steps[...].astype(jnp.float32).T
    for c in range(BLOCKS):
        buf[c, GROUP : GROUP + HALF] = folded[c % 2]
        mine = jnp.concatenate(
            [turned[c * OWN : (c + 1) * OWN], turned[HEADS + c * OWN : HEADS + (c + 1) * OWN]], axis=0
        )
        buf[c, GROUP + HALF :] = jnp.concatenate([mine, jnp.zeros_like(mine)], axis=1).astype(
            jnp.bfloat16
        )
    for c in range(BLOCKS):
        fetch(c).wait()
        send(c).start()
    for c in range(BLOCKS):
        send(c).wait()


def half_silu(h):
    return h + h * jnp.tanh(h)


def pieces(value):
    parts = []
    for _ in range(3):
        part = value.astype(jnp.bfloat16).astype(jnp.float32)
        parts.append(part)
        value = value - part
    return parts


def ssm_kernel(
    buf, other, cw, cb, rate, skip, y, ybuf, sent, raw, row_s, cum_s, dec_s, end_s, tot_s, fixed_s, x_s, c_s, bt_s, btb_s, st_s, carry_s
):
    f32, bf16 = jnp.float32, jnp.bfloat16
    tm = lax.axis_index("tm")
    n8 = BLOCKS * 8

    raw_steps = buf[:, GROUP + HALF :, :GROUP].astype(f32).reshape(n8, GROUP)
    z = jnp.exp(-jnp.abs(raw_steps))
    u = 1.0 + z
    log1p = jnp.where(u == 1.0, z, jnp.log(u) * (z / jnp.where(u == 1.0, 1.0, u - 1.0)))
    dt = jnp.maximum(raw_steps, 0.0) + log1p
    sub = lax.broadcasted_iota(jnp.int32, (8, GROUP), 0)
    rates = jnp.zeros((8, GROUP), f32)
    for k in range(8):
        rates = jnp.where(sub == k, rate[k // OWN, tm * OWN + k % OWN], rates)
    decay = (dt.reshape(BLOCKS, 8, GROUP) * (rates * (-LOG2E))[None]).reshape(n8, GROUP)
    ri = lax.broadcasted_iota(jnp.int32, (GROUP, GROUP), 0)
    ci = lax.broadcasted_iota(jnp.int32, (GROUP, GROUP), 1)
    sums = jnp.concatenate([(ri <= ci).astype(f32), (ri >= ci).astype(f32)], axis=1).astype(bf16)
    both = jnp.dot(
        jnp.concatenate(pieces(decay), axis=1).astype(bf16),
        jnp.concatenate([sums] * 3, axis=0),
        preferred_element_type=f32,
    )
    prefix, suffix = both[:, :GROUP], both[:, GROUP:]
    is_fwd = lax.broadcasted_iota(jnp.int32, (n8, GROUP), 0) % 8 < OWN
    cum = jnp.where(is_fwd, prefix, suffix)
    total = jnp.where(is_fwd[:, :1], prefix[:, GROUP - 1 :], suffix[:, :1])
    row = cum - jnp.log(dt) * LOG2E
    row_s[...] = -row
    cum_s[...] = cum
    dec_s[...] = jnp.exp2(cum)
    end_s[...] = jnp.exp2(total - row)
    tot_s[...] = jnp.broadcast_to(jnp.exp2(total), (n8, GROUP))

    low = lax.broadcasted_iota(jnp.int32, (GROUP, 128), 1) < HEADDIM
    sub128 = lax.broadcasted_iota(jnp.int32, (96, 128), 0)
    for k in range(12):
        if k < 8:
            chosen = (sub128 < 24) & (sub128 % 8 == k)
        else:
            d, p = divmod(k - 8, 2)
            head = d * OWN + 2 * p + jnp.where(low[:96], 0, 1)
            chosen = (sub128 >= 32) & (sub128 < 56) & (sub128 % 8 == head)
        fixed_s[k] = jnp.where(chosen, 1.0, 0.0).astype(bf16)

    for t in range(4):
        raw[t, 0:8] = jnp.zeros((8, 128), f32)
        raw[t, 8 + BLOCKS * GROUP :] = jnp.zeros((8, 128), f32)

    even = lax.rem(tm, 2) == 0

    def widen(i, _):
        at = pl.multiple_of(8 + i * GROUP, 8)
        for t in range(2):
            raw[t, pl.ds(at, GROUP)] = buf[i, :GROUP, t * 128 : (t + 1) * 128].astype(f32)
            near = buf[i, GROUP : GROUP + HALF, t * 128 : (t + 1) * 128].astype(f32)
            far = other[i, :, t * 128 : (t + 1) * 128].astype(f32)
            raw[2, pl.ds(at + t * HALF, HALF)] = jnp.where(even, near, far)
            raw[3, pl.ds(at + t * HALF, HALF)] = jnp.where(even, far, near)
        return 0

    lax.fori_loop(0, BLOCKS, widen, 0)

    def conv(t, i, d, taps, offset):
        sign = 1 if d == 0 else -1
        acc = offset
        for k in range(4):
            acc = acc + taps[k] * raw[t, pl.ds(i * GROUP + (8 + sign * (k - 3)), GROUP)]
        return half_silu(acc)

    def taps_of(d, lanes):
        return [cw[d, pl.ds(k, 1), lanes] * 0.5 for k in range(4)], cb[pl.ds(d, 1), lanes] * 0.5

    for d in range(2):
        taps, offset = taps_of(d, slice(INNER, INNER + 128))

        def convolve_bc(j, _):
            for e in range(UNROLL_BC):
                i = j * UNROLL_BC + e
                bc = conv(2 + d, i, d, taps, offset).astype(bf16).astype(f32)
                c_s[d, i] = jnp.where(low, pltpu.roll(bc, STATE, 1), bc).astype(bf16)
                turned = bc.T[:STATE]
                bt_s[d, i] = turned
                btb_s[d, i] = turned.astype(bf16)
            return 0

        lax.fori_loop(0, BLOCKS // UNROLL_BC, convolve_bc, 0)

    for p in range(OWN // 2):
        lanes = pl.ds(pl.multiple_of(tm * WIDE + p * 128, 128), 128)
        filters = [taps_of(d, lanes) for d in range(2)]

        def convolve(j, _):
            for e in range(UNROLL_X):
                i = j * UNROLL_X + e
                ends = end_s[pl.ds(pl.multiple_of(8 * i, 8), 8)]
                for d in range(2):
                    x = conv(p, i, d, *filters[d]).astype(bf16)
                    x_s[d, p, i] = x
                    k = d * OWN + 2 * p
                    turned = bt_s[d, i]
                    scaled = jnp.concatenate(
                        [turned * ends[k : k + 1], turned * ends[k + 1 : k + 2]], axis=0
                    ).astype(bf16)
                    state = jnp.dot(scaled, x, preferred_element_type=f32)
                    st_s[d, p, i] = jnp.where(low[:STATE], state[:STATE], state[STATE:])
            return 0

        lax.fori_loop(0, BLOCKS // UNROLL_X, convolve, 0)

    def scan(i, carries):
        new = []
        for d in range(2):
            at = i if d == 0 else BLOCKS - 1 - i
            rows = tot_s[pl.ds(pl.multiple_of(8 * at, 8), 8)]
            for p in range(OWN // 2):
                carry = carries[2 * d + p]
                high = carry.astype(bf16)
                lanes = slice(p * 128, (p + 1) * 128)
                carry_s[d, at, :STATE, lanes] = high
                carry_s[d, at, STATE:, lanes] = (carry - high.astype(f32)).astype(bf16)
                k = d * OWN + 2 * p
                keep = jnp.where(low[:1], rows[k : k + 1], rows[k + 1 : k + 2])
                new.append(keep * carry + st_s[d, p, at])
        return tuple(new)

    lax.fori_loop(0, BLOCKS, scan, tuple(jnp.zeros((STATE, 128), f32) for _ in range(4)))

    skips = []
    for d in range(2):
        for p in range(OWN // 2):
            at = tm * OWN + 2 * p
            skips.append(jnp.where(low[:1], skip[d, at], skip[d, at + 1]))
    sub32 = lax.broadcasted_iota(jnp.int32, (32, GROUP), 0)
    ones = jnp.where(sub32 < 24, 1.0, 0.0)
    blank = jnp.zeros((8, GROUP), f32)

    def one_block(i):
        at = pl.ds(pl.multiple_of(8 * i, 8), 8)
        left = jnp.concatenate(
            [ones, *pieces(cum_s[at]), blank, *pieces(dec_s[at]), blank, jnp.zeros((32, GROUP), f32)],
            axis=0,
        ).T.astype(bf16)
        rows = jnp.concatenate([*pieces(row_s[at]), blank], axis=0)
        right = []
        for k in range(12):
            part = jnp.where(sub32 % 8 == k, rows, 0.0) if k < 8 else jnp.zeros((32, GROUP), f32)
            right.append(jnp.concatenate([part.astype(bf16), fixed_s[k]], axis=0))
        grid = jnp.dot(left, jnp.concatenate(right, axis=1), preferred_element_type=f32)
        scores, wide = [], [0.0, 0.0]
        for d in range(2):
            c = c_s[d, i]
            score = jnp.dot(c[:, :STATE], btb_s[d, i], preferred_element_type=f32)
            scores.append(jnp.where((ri >= ci) if d == 0 else (ri <= ci), score, 0.0))
            carried = jnp.dot(c, carry_s[d, i], preferred_element_type=f32)
            for p in range(OWN // 2):
                lanes = slice(p * 128, (p + 1) * 128)
                decays = grid[:, (8 + 2 * d + p) * 128 : (9 + 2 * d + p) * 128]
                wide[p] = (
                    wide[p] + carried[:, lanes] * decays + skips[2 * d + p] * x_s[d, p, i].astype(f32)
                )
        for p in range(OWN // 2):
            heads = []
            for q in range(2):
                parts = []
                for d in range(2):
                    k = d * OWN + 2 * p + q
                    grow = jnp.exp2(jnp.minimum(grid[:, k * 128 : (k + 1) * 128], 64.0))
                    parts.append((grow * scores[d]).astype(bf16))
                heads.append(jnp.concatenate(parts, axis=1))
            local = jnp.dot(
                jnp.concatenate(heads, axis=0),
                jnp.concatenate([x_s[0, p, i], x_s[1, p, i]], axis=0),
                preferred_element_type=f32,
            )
            local = jnp.where(low, local[:GROUP], local[GROUP:])
            ybuf[i, :, p * 128 : (p + 1) * 128] = local + wide[p]

    def send(j):
        at = pl.ds(j * UNROLL_Y, UNROLL_Y)
        return pltpu.make_async_copy(ybuf.at[at], y.at[at], sent.at[j])

    def outputs(j, _):
        @pl.when(j > 0)
        def _():
            send(j - 1).start()

        for e in range(UNROLL_Y):
            one_block(j * UNROLL_Y + e)
        return 0

    count = BLOCKS // UNROLL_Y
    lax.fori_loop(0, count, outputs, 0)
    send(count - 1).start()
    for j in range(count):
        send(j).wait()


def gate_kernel(y, gate, gated, sums, out, wide, ybuf, came, sent):
    f32, bf16 = jnp.float32, jnp.bfloat16

    def fetch(j):
        at = pl.ds(j * 4, 4)
        return pltpu.make_async_copy(y.at[at], ybuf.at[at], came.at[j])

    def send(j):
        at = pl.ds(j * 4, 4)
        return pltpu.make_async_copy(out.at[at], gated.at[at], sent.at[j])

    for j in range(BLOCKS // 4):
        fetch(j).start()

    def four(j, _):
        @pl.when(j > 0)
        def _():
            send(j - 1).start()

        for e in range(4):
            i = j * 4 + e
            wide[i] = half_silu(gate[i].astype(f32) * 0.5)
        fetch(j).wait()
        for e in range(4):
            i = j * 4 + e
            g = ybuf[i] * wide[i]
            out[i] = g.astype(bf16)
            square = g * g
            square = square[:, :128] + square[:, 128:]
            high = square.astype(bf16)
            parts = jnp.concatenate([high, (square - high.astype(f32)).astype(bf16)], axis=1)
            total = lax.dot_general(
                jnp.ones((8, WIDE), bf16), parts, (((1,), (1,)), ((), ())), preferred_element_type=f32
            )
            sums[pl.ds(i, 1)] = total[:1]
        return 0

    lax.fori_loop(0, BLOCKS // 4, four, 0)
    send(BLOCKS // 4 - 1).start()
    for j in range(BLOCKS // 4):
        send(j).wait()


def norm_kernel(gated, total, gain, target, out, sent):
    gains = gain[0:1, pl.ds(pl.multiple_of(lax.axis_index("tm") * WIDE, WIDE), WIDE)]
    inv = lax.rsqrt(total[...] * (1.0 / INNER) + EPSILON)
    columns = jnp.concatenate([inv, jnp.zeros((GROUP - BLOCKS, GROUP), jnp.float32)], axis=0).T

    def send(j):
        at = pl.ds(j * 2, 2)
        return pltpu.make_async_copy(out.at[at], target.at[at], sent.at[j])

    for j in range(BLOCKS // 2):
        if j > 0:
            send(j - 1).start()
        for i in range(2 * j, 2 * j + 2):
            wide = gated[i].astype(jnp.float32) * columns[:, i : i + 1] * gains
            out[i] = wide.astype(jnp.bfloat16)
    send(BLOCKS // 2 - 1).start()
    for j in range(BLOCKS // 2):
        send(j).wait()


def total_of(sums):
    for moves in (
        [[i ^ b for i in range(BLOCKS)] for b in (1, 2, 3)],
        [[(i + b) % BLOCKS for i in range(BLOCKS)] for b in (4, 8, 12)],
    ):
        came = [lax.ppermute(sums, "tm", list(enumerate(move))) for move in moves]
        sums = sums + came[0] + came[1] + came[2]
    return sums


def turned_over(rows, bits):
    mine = lax.axis_index("batch")
    for b in bits:
        pairs = rows.reshape(BLOCKS >> (b + 1), 2, 1 << b, GROUP)
        upper = (mine >> b) & 1 == 1
        give = jnp.where(upper, pairs[:, 0], pairs[:, 1])
        got = lax.ppermute(give, "batch", [(i, i ^ (1 << b)) for i in range(BLOCKS)])
        pairs = [jnp.where(upper, got, pairs[:, 0]), jnp.where(upper, pairs[:, 1], got)]
        rows = jnp.stack(pairs, axis=1).reshape(BLOCKS, GROUP)
    return rows


def far(array):
    return pltpu.with_memory_space_constraint(array, pltpu.HBM)


def local(array):
    return pltpu.with_memory_space_constraint(array, pltpu.VMEM)


def swap(array, axis):
    return lax.all_to_all(array, axis, split_axis=0, concat_axis=0, tiled=True)


def shards(
    signal,
    gate_input,
    bc_forward,
    bc_backward,
    step_raw,
    decay_rate,
    conv_weight,
    conv_bias,
    skip_gain,
    norm_gain,
):
    f32, bf16 = jnp.float32, jnp.bfloat16
    packed = pl.pallas_call(
        pack_kernel,
        out_shape=pltpu.HBM((BLOCKS, ROWS, WIDE), bf16),
        in_specs=[ANY] * 4,
        out_specs=ANY,
        scratch_shapes=[
            pltpu.VMEM((BLOCKS, ROWS, WIDE), bf16),
            pltpu.VMEM((2, GROUP, 128), bf16),
            pltpu.VMEM((GROUP, 128), bf16),
            pltpu.SemaphoreType.DMA((BLOCKS,)),
            pltpu.SemaphoreType.DMA((3,)),
            pltpu.SemaphoreType.DMA((BLOCKS,)),
        ],
        name="pack",
        cost_estimate=pl.CostEstimate(flops=0, bytes_accessed=3 << 20, transcendentals=0),
    )(*[far(a) for a in (signal, bc_forward, bc_backward, step_raw)])
    gates = gate_input[0].reshape(GROUP, BLOCKS, WIDE).transpose(1, 0, 2)
    got, gates = lax.optimization_barrier((swap(packed, "tm"), gates))
    other = lax.ppermute(
        got[:, GROUP : GROUP + HALF], "tm", [(i, i ^ 1) for i in range(BLOCKS)]
    )
    gates = swap(gates, "tm")
    y = pl.pallas_call(
        ssm_kernel,
        out_shape=pltpu.HBM((BLOCKS, GROUP, WIDE), f32),
        compiler_params=LIMIT,
        in_specs=[VMEM, VMEM, VMEM, VMEM, SMEM, SMEM],
        out_specs=ANY,
        scratch_shapes=[
            pltpu.VMEM((BLOCKS, GROUP, WIDE), f32),
            pltpu.SemaphoreType.DMA((BLOCKS // UNROLL_Y,)),
            pltpu.VMEM((4, BLOCKS * GROUP + 16, 128), f32),
            *[pltpu.VMEM((BLOCKS * 8, GROUP), f32)] * 5,
            pltpu.VMEM((12, 96, 128), bf16),
            pltpu.VMEM((2, 2, BLOCKS, GROUP, 128), bf16),
            pltpu.VMEM((2, BLOCKS, GROUP, 128), bf16),
            pltpu.VMEM((2, BLOCKS, STATE, 128), f32),
            pltpu.VMEM((2, BLOCKS, STATE, 128), bf16),
            pltpu.VMEM((2, 2, BLOCKS, STATE, 128), f32),
            pltpu.VMEM((2, BLOCKS, 2 * STATE, WIDE), bf16),
        ],
        name="ssm",
        cost_estimate=pl.CostEstimate(
            flops=20_000_000_000, bytes_accessed=8 << 20, transcendentals=4_000_000
        ),
    )(local(got), local(other), conv_weight, conv_bias, decay_rate, skip_gain)
    gated, sums = pl.pallas_call(
        gate_kernel,
        out_shape=(
            pltpu.HBM((BLOCKS, GROUP, WIDE), bf16),
            pltpu.VMEM((BLOCKS, GROUP), f32),
        ),
        compiler_params=LIMIT,
        in_specs=[ANY, VMEM],
        out_specs=(ANY, VMEM),
        scratch_shapes=[
            pltpu.VMEM((BLOCKS, GROUP, WIDE), bf16),
            pltpu.VMEM((BLOCKS, GROUP, WIDE), f32),
            pltpu.VMEM((BLOCKS, GROUP, WIDE), f32),
            pltpu.SemaphoreType.DMA((BLOCKS // 4,)),
            pltpu.SemaphoreType.DMA((BLOCKS // 4,)),
        ],
        name="gate",
    )(far(y), local(gates))
    sums = turned_over(sums, EARLY)
    gated = swap(gated, "batch")
    sums = total_of(sums)
    sums = turned_over(sums, LATE)
    return pl.pallas_call(
        norm_kernel,
        out_shape=pltpu.HBM((BLOCKS, GROUP, WIDE), bf16),
        in_specs=[VMEM] * 3,
        out_specs=ANY,
        scratch_shapes=[
            pltpu.VMEM((BLOCKS, GROUP, WIDE), bf16),
            pltpu.SemaphoreType.DMA((BLOCKS // 2,)),
        ],
        compiler_params=LIMIT,
        name="norm",
    )(local(gated), sums, norm_gain[None])


def solution(mesh):
    in_specs = (
        P("batch", "tm", None),
        P("batch", "tm", None),
        P("batch", "tm", None),
        P("batch", "tm", None),
        P("batch", "tm", None),
        P(),
        P(),
        P(),
        P(),
        P(),
    )
    out_specs = P(None, "batch", "tm")
    return jax.shard_map(shards, mesh=mesh, in_specs=in_specs, out_specs=out_specs, check_vma=False)
```
